32 devices in a mesh: dp: 8 (over z, y), tensor: 4 (over x, core).
Axes of the slice: x: 2, y: 2, z: 4, core: 2. Of those that a mesh axis runs over, the one named last changes fastest.
Arguments:
- hidden: bfloat16 [16384, 768], P('dp'), may hold values from -6 to 6
- cotangent: bfloat16 [16384, 768], P('dp'), may hold values from -6 to 6
- seg_ids: int32 [16384], P('dp'), may hold values from 0 to 1024, as said below
- counts: int32 [8], P('dp'), may hold values from 1024 to 2048, as said below
- norm_gain: float32 [768], replicated, may hold values from 0.5 to 1.5
- w_x: bfloat16 [768, 1536], P(None, 'tensor'), may hold values from -0.21875 to 0.21875
- w_z: bfloat16 [768, 1536], P(None, 'tensor'), may hold values from -0.21875 to 0.21875
- w_dt: bfloat16 [768, 24], P(None, 'tensor'), may hold values from -0.21875 to 0.21875
- w_bc: bfloat16 [768, 256], replicated, may hold values from -0.21875 to 0.21875
- conv_x: float32 [4, 1536], P(None, 'tensor'), may hold values from -3 to 3
- conv_x_bias: float32 [1536], P('tensor'), may hold values from -0.5 to 0.5
- conv_bc: float32 [4, 256], replicated, may hold values from -3 to 3
- conv_bc_bias: float32 [256], replicated, may hold values from -0.5 to 0.5
- dt_bias: float32 [24], P('tensor'), may hold values from -4 to -1
- a_log: float32 [24], P('tensor'), may hold values from -1 to 2.5
- d_skip: float32 [24], P('tensor'), may hold values from 0.5 to 1.5
- gate_gain: float32 [1536], P('tensor'), may hold values from 0.5 to 1.5
- w_out: bfloat16 [1536, 768], P('tensor'), may hold values from -0.15625 to 0.15625
Outputs:
- block_out: bfloat16 [16384, 768], P('dp')
- grad_hidden: float32 [16384, 768], P('dp')
- grad_norm_gain: float32 [768], replicated
- grad_w_x: float32 [768, 1536], P(None, 'tensor')
- grad_w_z: float32 [768, 1536], P(None, 'tensor')
- grad_w_dt: float32 [768, 24], P(None, 'tensor')
- grad_w_bc: float32 [768, 256], replicated
- grad_conv_x: float32 [4, 1536], P(None, 'tensor')
- grad_conv_x_bias: float32 [1536], P('tensor')
- grad_conv_bc: float32 [4, 256], replicated
- grad_conv_bc_bias: float32 [256], replicated
- grad_dt_bias: float32 [24], P('tensor')
- grad_a_log: float32 [24], P('tensor')
- grad_d_skip: float32 [24], P('tensor')
- grad_gate_gain: float32 [1536], P('tensor')
- grad_w_out: float32 [1536, 768], P('tensor')
The draws below stay inside these ranges and needn't reach their ends.
Inputs may be any that keep to these rules, and one draw needn't show every extreme that they name: `seg_ids`: within each shard of 2048 slots the ids start at 0, never fall and rise by at most 1 from slot to slot; slots 0 to 1023 have id 0 and slot 1024 starts a new id; in some shard every slot from 1024 on starts a new id. `counts`: each shard's count is at least 1024; some shard is full in every draw.
All inputs are finite; a program needn't handle non-finite values.
Results may differ from the reference program's by a relative error of at most 0.012.
Values sent between devices are 32-bit elements; how exact they have to be, the bound alone decides.
No kernel may reach another device: no remote copies, remote signals or barrier semaphores. Data moves between devices by JAX's collectives and lax.ppermute only.
A program may use at most 128 MiB of HBM per device.

```python
import jax
import jax.numpy as jnp
from jax import lax

D = 768
INNER = 1536
HEADS = 24
HEAD = 64
STATE = 128
KCONV = 4
SPAN = 256
TOK_DEV = 2048
FIRST_SEG = 1024
TOKENS = 16384
N_DP = 8


def shard_layout(key):
    shards = TOKENS // TOK_DEV
    count_key, full_key, start_key, short_key = jax.random.split(jax.random.fold_in(key, 11), 4)
    drawn_counts = jax.random.randint(count_key, (shards,), TOK_DEV // 2, TOK_DEV + 1)
    fullest = jax.random.randint(full_key, (), 0, shards)
    drawn_counts = jnp.where(jnp.arange(shards) == fullest, TOK_DEV, drawn_counts).astype(jnp.int32)
    coin_flips = jax.random.randint(start_key, (shards, TOK_DEV), 0, 96)
    positions = jnp.arange(TOK_DEV)[None, :]
    starts = jnp.where(positions < FIRST_SEG, 0, (coin_flips == 0).astype(jnp.int32))
    starts = jnp.where(positions == FIRST_SEG, 1, starts)
    busiest = jax.random.randint(short_key, (), 0, shards)
    many_docs = (jnp.arange(shards)[:, None] == busiest) & (positions >= FIRST_SEG)
    starts = jnp.where(many_docs, 1, starts)
    ids_drawn = jnp.cumsum(starts, axis=1).astype(jnp.int32)
    return (drawn_counts, ids_drawn.reshape(TOKENS))


def draw_seg_ids(key, part):
    return shard_layout(key)[1]


def draw_counts(key, part):
    return shard_layout(key)[0]


def shard_levels(rng, shape, pieces, smallest, largest):
    factor_of, own = 1.0, jax.random.fold_in(rng, 6)
    for position, shards_of in pieces:
        steps = jnp.exp(jax.random.uniform(jax.random.fold_in(own, position), (shards_of,), jnp.float32, smallest / len(pieces), largest / len(pieces)))
        factor_of = factor_of * jnp.repeat(steps, shape[position] // shards_of).reshape([-1 if axis == position else 1 for axis in range(len(shape))])
    return factor_of


def normal_values(stream_key, dims, spread, most, cuts=(), kind=jnp.bfloat16):
    gain = shard_levels(stream_key, dims, cuts, -0.22, 0.18) if cuts else 1.0
    entries = jax.random.normal(stream_key, dims, jnp.float32) * spread * gain
    return jnp.minimum(jnp.maximum(entries, -most), most).astype(kind)


def setup_inputs(seed: int = 0) -> dict:
    splits = jax.random.split(jax.random.key(seed), 19)
    return {
        "hidden": normal_values(splits[0], (TOKENS, D), 1.0, 6.0, ((0, 8),)),
        "cotangent": normal_values(splits[1], (TOKENS, D), 1.0, 6.0, ((0, 8),)),
        "seg_ids": draw_seg_ids(jax.random.fold_in(splits[18], 71), 0),
        "counts": draw_counts(jax.random.fold_in(splits[18], 71), 0),
        "norm_gain": jnp.clip(1.0 + 0.1 * jax.random.normal(splits[4], (D,), jnp.float32), 0.5, 1.5),
        "w_x": normal_values(splits[5], (D, INNER), D ** -0.5, 0.21875, ((1, 4),)),
        "w_z": normal_values(splits[6], (D, INNER), D ** -0.5, 0.21875, ((1, 4),)),
        "w_dt": normal_values(splits[7], (D, HEADS), D ** -0.5, 0.21875, ((1, 4),)),
        "w_bc": normal_values(splits[8], (D, 2 * STATE), D ** -0.5, 0.21875),
        "conv_x": normal_values(splits[9], (KCONV, INNER), 0.5, 3.0, ((1, 4),), jnp.float32),
        "conv_x_bias": jnp.clip(jax.random.uniform(splits[10], (INNER,), jnp.float32, -0.5, 0.5) * shard_levels(splits[10], (INNER,), ((0, 4),), -0.4, 0.0), -0.5, 0.5),
        "conv_bc": normal_values(splits[11], (KCONV, 2 * STATE), 0.5, 3.0, (), jnp.float32),
        "conv_bc_bias": jnp.clip(jax.random.uniform(splits[12], (2 * STATE,), jnp.float32, -0.5, 0.5), -0.5, 0.5),
        "dt_bias": jnp.clip(-4.0 + 3.0 * jax.random.uniform(splits[13], (HEADS,), jnp.float32) ** shard_levels(splits[13], (HEADS,), ((0, 4),), -0.2, 0.2), -4.0, -1.0),
        "a_log": jnp.clip(-1.0 + 3.5 * jax.random.uniform(splits[14], (HEADS,), jnp.float32) ** shard_levels(splits[14], (HEADS,), ((0, 4),), -0.2, 0.2), -1.0, 2.5),
        "d_skip": jnp.clip(0.5 + 1.0 * jax.random.uniform(splits[15], (HEADS,), jnp.float32) ** shard_levels(splits[15], (HEADS,), ((0, 4),), -0.2, 0.2), 0.5, 1.5),
        "gate_gain": jnp.clip(1.0 + 0.1 * jax.random.normal(splits[16], (INNER,), jnp.float32), 0.5, 1.5),
        "w_out": normal_values(splits[17], (INNER, D), INNER ** -0.5, 0.15625, ((0, 4),)),
    }


EPS = 1e-05

@jax.custom_vjp
def low(v):
    return lax.optimization_barrier(v.astype(jnp.bfloat16)).astype(jnp.float32)

@jax.custom_vjp
def low_back(v):
    return v

def low_keep(v):
    return (low(v), None)

def low_pass(kept, grad):
    return (grad,)

def back_keep(v):
    return (v, None)

def back_low(kept, grad):
    return (low(grad),)
low.defvjp(low_keep, low_pass)
low_back.defvjp(back_keep, back_low)

def matmul(left, right):
    return jnp.dot(left, right, precision=lax.Precision.HIGHEST, preferred_element_type=jnp.float32)

def conv_apply(values, weight, bias, seg_here):
    length = values.shape[0]
    positions = jnp.arange(length)
    total = bias + weight[0] * values
    for offset in range(1, KCONV):
        earlier = jnp.concatenate([jnp.zeros((offset, values.shape[1]), values.dtype), values[:-offset]], 0)
        seg_before = jnp.concatenate([jnp.zeros((offset,), jnp.int32), seg_here[:-offset]], 0)
        keeping = ((seg_before == seg_here) & (positions >= offset)).astype(values.dtype)
        total = total + weight[offset] * earlier * keeping[:, None]
    return total

def span_scan(c_low, b_low, inputs, log_decay, seg_here):
    span_count = TOK_DEV // SPAN
    highest = lax.Precision.HIGHEST
    ld_blocks = log_decay.reshape(span_count, SPAN, HEADS)
    seg_blocks = seg_here.reshape(span_count, SPAN)
    local_pos = jnp.arange(SPAN)
    intra = (local_pos[:, None] >= local_pos[None, :])[None] & (seg_blocks[:, :, None] == seg_blocks[:, None, :])
    ld_heads = jnp.transpose(ld_blocks, (0, 2, 1))
    exponent = jnp.where(intra[:, None], ld_heads[:, :, :, None] - ld_heads[:, :, None, :], -10000.0)
    b_blocks = b_low.reshape(span_count, SPAN, STATE)
    c_blocks = c_low.reshape(span_count, SPAN, STATE)
    inputs_blocks = inputs.reshape(span_count, SPAN, HEADS, HEAD)
    kernel_small = jnp.einsum('cpn,cqn->cpq', c_blocks, b_blocks, precision=highest)
    kernel = low_back(jnp.broadcast_to(kernel_small[:, None], (span_count, HEADS, SPAN, SPAN)))
    mixing = low(kernel * jnp.exp(exponent))
    local_part = jnp.einsum('chpq,cqhd->cphd', mixing, inputs_blocks, precision=highest)
    ld_end = ld_blocks[:, -1]
    seg_end = seg_blocks[:, -1]
    in_keep = (seg_blocks == seg_end[:, None])[:, :, None]
    decay_in = jnp.where(in_keep, jnp.exp(ld_end[:, None, :] - ld_blocks), 0.0)
    weighted_b = low(b_blocks[:, :, None, :] * decay_in[..., None])
    span_new = jnp.einsum('cqhn,cqhd->chnd', weighted_b, inputs_blocks, precision=highest)
    hop = jnp.where((seg_end[1:] == seg_end[:-1])[:, None], jnp.exp(ld_end[1:] - ld_end[:-1]), 0.0)
    state = jnp.zeros((HEADS, STATE, HEAD), jnp.float32)
    befores = []
    for span in range(span_count):
        befores.append(state)
        if span == 0:
            state = span_new[0]
        else:
            state = hop[span - 1][:, None, None] * state + span_new[span]
    carried = low(jnp.stack(befores, 0))
    prev_seg = jnp.concatenate([jnp.full((1,), -1, jnp.int32), seg_end[:-1].astype(jnp.int32)], 0)
    prev_ld = jnp.concatenate([jnp.zeros((1, HEADS), jnp.float32), ld_end[:-1]], 0)
    out_keep = (seg_blocks == prev_seg[:, None])[:, :, None]
    decay_out = jnp.where(out_keep, jnp.exp(ld_blocks - prev_ld[:, None, :]), 0.0)
    cross_raw = jnp.einsum('cpn,chnd->cphd', c_blocks, carried, precision=highest)
    return (local_part + decay_out[..., None] * cross_raw).reshape(TOK_DEV, HEADS, HEAD)

def shard_mix(hidden_rows, seg_here, count_here, weights):
    norm_gain, w_x, w_z, w_dt, w_bc, conv_x, conv_x_bias, conv_bc, conv_bc_bias, dt_bias, a_log, d_skip, gate_gain, w_out = weights
    positions = jnp.arange(TOK_DEV)
    live_rows = (positions < count_here).astype(hidden_rows.dtype)
    inv_rms = lax.rsqrt(lax.optimization_barrier(jnp.mean(hidden_rows * hidden_rows, -1, keepdims=True)) + EPS)
    normed = low(hidden_rows * inv_rms * norm_gain)
    proj_x = low_back(matmul(normed, w_x))
    proj_z = low_back(matmul(normed, w_z))
    proj_dt = matmul(normed, w_dt)
    proj_bc = matmul(normed, w_bc)
    x_conv = jax.nn.silu(conv_apply(proj_x, conv_x, conv_x_bias, seg_here))
    bc_conv = jax.nn.silu(conv_apply(proj_bc, conv_bc, conv_bc_bias, seg_here))
    b_low = low(bc_conv[:, :STATE])
    c_low = low(bc_conv[:, STATE:])
    step_size = jax.nn.softplus(proj_dt + dt_bias)
    log_decay = jnp.cumsum(step_size * -jnp.exp(a_log), 0)
    x_heads = x_conv.reshape(TOK_DEV, HEADS, HEAD)
    inputs = low(step_size[:, :, None] * x_heads)
    scanned = low_back(span_scan(c_low, b_low, inputs, log_decay, seg_here))
    y_flat = (scanned + d_skip[None, :, None] * x_heads).reshape(TOK_DEV, INNER)
    gated_out = y_flat * jax.nn.silu(proj_z)
    inv_gate = lax.rsqrt(lax.optimization_barrier(jnp.mean(gated_out * gated_out, -1, keepdims=True)) + EPS)
    out_in = low(gated_out * inv_gate * gate_gain)
    return hidden_rows + live_rows[:, None] * matmul(out_in, w_out)

def reference(hidden, cotangent, seg_ids, counts, norm_gain, w_x, w_z, w_dt, w_bc, conv_x, conv_x_bias, conv_bc, conv_bc_bias, dt_bias, a_log, d_skip, gate_gain, w_out):
    segments = seg_ids.reshape(N_DP, TOK_DEV)

    def forward(hidden_wide, gain_one, wx_wide, wz_wide, wdt_wide, wbc_wide, convx_one, convxb_one, convbc_one, convbcb_one, dtb_one, alog_one, skip_one, gate_one, wout_wide):
        weights = (gain_one, wx_wide, wz_wide, wdt_wide, wbc_wide, convx_one, convxb_one, convbc_one, convbcb_one, dtb_one, alog_one, skip_one, gate_one, wout_wide)

        def one_shard(shard_item):
            return shard_mix(shard_item[0], shard_item[1], shard_item[2], weights)
        stacked = lax.map(jax.checkpoint(one_shard), (hidden_wide.reshape(N_DP, TOK_DEV, D), segments, counts))
        return stacked.reshape(TOKENS, D)
    output, pullback = jax.vjp(forward, hidden.astype(jnp.float32), norm_gain, w_x.astype(jnp.float32), w_z.astype(jnp.float32), w_dt.astype(jnp.float32), w_bc.astype(jnp.float32), conv_x, conv_x_bias, conv_bc, conv_bc_bias, dt_bias, a_log, d_skip, gate_gain, w_out.astype(jnp.float32))
    grads = pullback(cotangent.astype(jnp.float32))
    return (output.astype(jnp.bfloat16), grads[0], grads[1], grads[2], grads[3], grads[4], grads[5], grads[6], grads[7], grads[8], grads[9], grads[10], grads[11], grads[12], grads[13], grads[14])
```

```python
import functools

import jax
import jax.numpy as jnp
from jax import lax
from jax.sharding import PartitionSpec as P

INNER = 1536
SPAN = 256


EPS = 1e-05


def silu_grad(values):
    sigmoid_of = jax.nn.sigmoid(values)
    return sigmoid_of * (1.0 + values * (1.0 - sigmoid_of))


def lagged(values, offset):
    if offset == 0:
        return values
    padding = jnp.zeros((offset,) + values.shape[1:], values.dtype)
    return jnp.concatenate([padding, values[:-offset]], 0)


def leading(values, offset):
    padding = jnp.zeros((offset,) + values.shape[1:], values.dtype)
    return jnp.concatenate([values[offset:], padding], 0)


def conv_apply(values, weight, bias, conv_masks):
    total = bias + weight[0] * values
    for offset in range(1, len(conv_masks)):
        total = total + weight[offset] * lagged(values, offset) * conv_masks[offset]
    return total


def conv_back(values, weight, conv_masks, grad_pre):
    grad_weight = jnp.stack(
        [
            jnp.sum(grad_pre * conv_masks[offset] * lagged(values, offset), 0)
            for offset in range(len(conv_masks))
        ],
        0,
    )
    grad_bias = jnp.sum(grad_pre, 0)
    grad_values = grad_pre * weight[0]
    for offset in range(1, len(conv_masks)):
        grad_values = grad_values + leading(grad_pre * conv_masks[offset], offset) * weight[offset]
    return (grad_weight, grad_bias, grad_values)


def partners(count, step):
    return [(place, place ^ step) for place in range(count)]


def steps_of(count):
    return [1 << level for level in range((count - 1).bit_length())]


def axis_sum_small(values, axis, count):
    for step in steps_of(count):
        values = values + lax.ppermute(values, axis, partners(count, step))
    return values


def take_half(values, which):
    half = values.shape[0] // 2
    return lax.dynamic_slice_in_dim(values, which * half, half, 0)


def axis_scatter(values, axis, count, order):
    place = lax.axis_index(axis)
    for step in order:
        mine = (place // step) % 2
        sent = lax.ppermute(take_half(values, 1 - mine), axis, partners(count, step))
        values = take_half(values, mine) + sent
    return values


def axis_gather(values, axis, count, order):
    place = lax.axis_index(axis)
    for step in reversed(order):
        mine = (place // step) % 2
        other = lax.ppermute(values, axis, partners(count, step))
        values = join_halves(values, other, mine)
    return values


def join_halves(own, other, mine):
    return jnp.where(
        mine == 0, jnp.concatenate([own, other], 0), jnp.concatenate([other, own], 0)
    )


def dp_sum(values, count, first):
    order = steps_of(count)
    order = order[first:2] + order[:first] + order[2:]
    return axis_gather(axis_scatter(values, "dp", count, order), "dp", count, order)


def wide_tensor_sum(compute, count):
    mine = lax.axis_index("tensor") % 2
    values = compute(mine) + lax.ppermute(compute(1 - mine), "tensor", partners(count, 1))
    for step in steps_of(count)[1:]:
        values = values + lax.ppermute(values, "tensor", partners(count, step))
    return values, lax.ppermute(values, "tensor", partners(count, 1)), mine


def pad_rows(values, multiple):
    missing = -values.shape[0] % multiple
    return jnp.pad(values, ((0, missing), (0, 0)))


def per_device(
    n_dp,
    n_tensor,
    hidden,
    cotangent,
    seg_ids,
    counts,
    norm_gain,
    w_x,
    w_z,
    w_dt,
    w_bc,
    conv_x,
    conv_x_bias,
    conv_bc,
    conv_bc_bias,
    dt_bias,
    a_log,
    d_skip,
    gate_gain,
    w_out,
):
    row_count = hidden.shape[0]
    state_width = w_bc.shape[1] // 2
    heads_here = w_dt.shape[1]
    width_here = w_x.shape[1]
    head_size = width_here // heads_here
    tap_count = conv_x.shape[0]
    span_count = row_count // SPAN
    highest = lax.Precision.HIGHEST
    positions = jnp.arange(row_count)
    live_rows = (positions < counts[0]).astype(jnp.float32)[:, None]
    conv_masks = [
        ((lagged(seg_ids, offset) == seg_ids) & (positions >= offset)).astype(jnp.float32)[:, None]
        for offset in range(tap_count)
    ]
    hidden_wide = hidden.astype(jnp.float32)
    inv_rms = lax.rsqrt(jnp.mean(hidden_wide * hidden_wide, -1, keepdims=True) + EPS)
    normed = (hidden_wide * inv_rms * norm_gain).astype(jnp.bfloat16)
    normed_wide = normed.astype(jnp.float32)
    proj_x = jnp.dot(normed, w_x, preferred_element_type=jnp.float32)
    proj_z = jnp.dot(normed, w_z, preferred_element_type=jnp.float32)
    proj_dt = jnp.dot(normed, w_dt, preferred_element_type=jnp.float32)
    proj_bc = jnp.dot(normed, w_bc, preferred_element_type=jnp.float32)
    x_pre = conv_apply(proj_x, conv_x, conv_x_bias, conv_masks)
    bc_pre = conv_apply(proj_bc, conv_bc, conv_bc_bias, conv_masks)
    x_conv = jax.nn.silu(x_pre)
    bc_conv = jax.nn.silu(bc_pre)
    b_low = bc_conv[:, :state_width].astype(jnp.bfloat16)
    c_low = bc_conv[:, state_width:].astype(jnp.bfloat16)
    dt_in = proj_dt + dt_bias
    step_size = jax.nn.softplus(dt_in)
    rates = -jnp.exp(a_log)
    log_decay = jnp.cumsum(step_size * rates, 0)
    x_heads = x_conv.reshape(row_count, heads_here, head_size)
    inputs = (step_size[:, :, None] * x_heads).astype(jnp.bfloat16)
    ld_blocks = log_decay.reshape(span_count, SPAN, heads_here)
    seg_blocks = seg_ids.reshape(span_count, SPAN)
    local_pos = jnp.arange(SPAN)
    intra = (local_pos[:, None] >= local_pos[None, :])[None] & (
        seg_blocks[:, :, None] == seg_blocks[:, None, :]
    )
    ld_heads = jnp.transpose(ld_blocks, (0, 2, 1))
    exponent = jnp.where(
        intra[:, None], ld_heads[:, :, :, None] - ld_heads[:, :, None, :], -10000.0
    )
    decays = jnp.exp(exponent)
    b_blocks = b_low.reshape(span_count, SPAN, state_width)
    c_blocks = c_low.reshape(span_count, SPAN, state_width)
    inputs_blocks = inputs.reshape(span_count, SPAN, heads_here, head_size)
    kernel = jnp.einsum("cpn,cqn->cpq", c_blocks, b_blocks, preferred_element_type=jnp.float32)
    mixing = (kernel[:, None] * decays).astype(jnp.bfloat16)
    local_part = jnp.einsum(
        "chpq,cqhd->cphd", mixing, inputs_blocks, preferred_element_type=jnp.float32
    )
    ld_end = ld_blocks[:, -1]
    seg_end = seg_blocks[:, -1]
    in_keep = (seg_blocks == seg_end[:, None])[:, :, None]
    decay_in = jnp.where(in_keep, jnp.exp(ld_end[:, None, :] - ld_blocks), 0.0)
    b_blocks_wide = b_blocks.astype(jnp.float32)
    weighted_b = (b_blocks_wide[:, :, None, :] * decay_in[..., None]).astype(jnp.bfloat16)
    span_new = jnp.einsum(
        "cqhn,cqhd->chnd", weighted_b, inputs_blocks, preferred_element_type=jnp.float32
    )
    hop = jnp.where((seg_end[1:] == seg_end[:-1])[:, None], jnp.exp(ld_end[1:] - ld_end[:-1]), 0.0)
    state = jnp.zeros((heads_here, state_width, head_size), jnp.float32)
    befores = []
    for span in range(span_count):
        befores.append(state)
        if span == 0:
            state = span_new[0]
        else:
            state = hop[span - 1][:, None, None] * state + span_new[span]
    states_before = jnp.stack(befores, 0)
    carried_low = states_before.astype(jnp.bfloat16)
    prev_seg = jnp.concatenate([jnp.full((1,), -1, jnp.int32), seg_end[:-1]], 0)
    prev_ld = jnp.concatenate([jnp.zeros((1, heads_here), jnp.float32), ld_end[:-1]], 0)
    out_keep = (seg_blocks == prev_seg[:, None])[:, :, None]
    decay_out = jnp.where(out_keep, jnp.exp(ld_blocks - prev_ld[:, None, :]), 0.0)
    cross_raw = jnp.einsum(
        "cpn,chnd->cphd", c_blocks, carried_low, preferred_element_type=jnp.float32
    )
    scanned = (local_part + decay_out[..., None] * cross_raw).reshape(
        row_count, heads_here, head_size
    )
    y_flat = (scanned + d_skip[None, :, None] * x_heads).reshape(row_count, width_here)
    z_active = jax.nn.silu(proj_z)
    gated_out = y_flat * z_active
    grad_out = cotangent.astype(jnp.float32)
    grad_mix = (live_rows * grad_out).astype(jnp.bfloat16)
    grad_in = jnp.dot(grad_mix, w_out.T, preferred_element_type=jnp.float32)
    grad_scaled = grad_in * gate_gain
    row_sums = axis_sum_small(
        jnp.stack([jnp.sum(gated_out * gated_out, -1), jnp.sum(grad_scaled * gated_out, -1)], 0),
        "tensor",
        n_tensor,
    )
    squares, cross_sum = row_sums[0], row_sums[1]
    inv_gate = lax.rsqrt(squares[:, None] / INNER + EPS)
    scaled = gated_out * inv_gate
    out_in = (scaled * gate_gain).astype(jnp.bfloat16)
    half_rows = row_count // 2

    def mixed_half(which):
        rows = lax.dynamic_slice_in_dim(out_in, which * half_rows, half_rows, 0)
        return jnp.dot(rows, w_out, preferred_element_type=jnp.float32)

    mixed = join_halves(*wide_tensor_sum(mixed_half, n_tensor))
    output = (hidden_wide + live_rows * mixed).astype(jnp.bfloat16)
    grad_w_out = dp_sum(
        jnp.dot(out_in.T, grad_mix, preferred_element_type=jnp.float32), n_dp, 0
    )
    grad_gate_gain = jnp.sum(grad_in * scaled, 0)
    grad_gated = inv_gate * grad_scaled - gated_out * inv_gate**3 * cross_sum[:, None] / INNER
    grad_y = (grad_gated * z_active).reshape(row_count, heads_here, head_size)
    grad_z = (grad_gated * y_flat * silu_grad(proj_z)).astype(jnp.bfloat16)
    grad_d_skip = jnp.sum(grad_y * x_heads, (0, 2))
    grad_scan = grad_y.astype(jnp.bfloat16)
    grad_scan_blocks = grad_scan.reshape(span_count, SPAN, heads_here, head_size)
    grad_mixing = jnp.einsum(
        "cphd,cqhd->chpq", grad_scan_blocks, inputs_blocks, preferred_element_type=jnp.float32
    )
    grad_inputs_blocks = jnp.einsum(
        "chpq,cphd->cqhd", mixing, grad_scan_blocks, preferred_element_type=jnp.float32
    )
    grad_kernel = (grad_mixing * decays).astype(jnp.bfloat16)
    grad_expo = grad_mixing * kernel[:, None] * decays
    grad_ld = jnp.transpose(jnp.sum(grad_expo, 3) - jnp.sum(grad_expo, 2), (0, 2, 1))
    grad_c_blocks = jnp.einsum(
        "chpq,cqn->cpn", grad_kernel, b_blocks, preferred_element_type=jnp.float32
    )
    grad_b_blocks = jnp.einsum(
        "chpq,cpn->cqn", grad_kernel, c_blocks, preferred_element_type=jnp.float32
    )
    grad_scan_wide = grad_scan_blocks.astype(jnp.float32)
    grad_decay_out = jnp.sum(grad_scan_wide * cross_raw, -1)
    grad_cross_raw = decay_out[..., None] * grad_scan_wide
    grad_c_blocks = grad_c_blocks + jnp.einsum(
        "cphd,chnd->cpn",
        grad_cross_raw,
        carried_low.astype(jnp.float32),
        precision=highest,
        preferred_element_type=jnp.float32,
    )
    grad_states = jnp.einsum(
        "cpn,cphd->chnd",
        c_blocks.astype(jnp.float32),
        grad_cross_raw,
        precision=highest,
        preferred_element_type=jnp.float32,
    )
    out_term = grad_decay_out * decay_out
    grad_ld = grad_ld + out_term
    grad_prev_ld = -jnp.sum(out_term, 1)
    grad_end = jnp.concatenate([grad_prev_ld[1:], jnp.zeros((1, heads_here), jnp.float32)], 0)
    flow = jnp.zeros((heads_here, state_width, head_size), jnp.float32)
    grad_new_list = [flow] * span_count
    hop_grads = []
    for span in reversed(range(span_count)):
        grad_new_list[span] = flow
        if span > 0:
            hop_grads.append(jnp.sum(flow * states_before[span], (1, 2)))
            flow = grad_states[span] + hop[span - 1][:, None, None] * flow
    grad_new = jnp.stack(grad_new_list, 0)
    hop_terms = jnp.stack(hop_grads[::-1], 0) * hop
    zero_row = jnp.zeros((1, heads_here), jnp.float32)
    grad_end = (
        grad_end
        + jnp.concatenate([zero_row, hop_terms], 0)
        - jnp.concatenate([hop_terms, zero_row], 0)
    )
    grad_weighted_b = jnp.einsum(
        "chnd,cqhd->cqhn",
        grad_new,
        inputs_blocks.astype(jnp.float32),
        precision=highest,
        preferred_element_type=jnp.float32,
    )
    grad_inputs_blocks = grad_inputs_blocks + jnp.einsum(
        "chnd,cqhn->cqhd",
        grad_new,
        weighted_b.astype(jnp.float32),
        precision=highest,
        preferred_element_type=jnp.float32,
    )
    grad_b_blocks = grad_b_blocks + jnp.sum(grad_weighted_b * decay_in[..., None], 2)
    in_term = jnp.sum(grad_weighted_b * b_blocks_wide[:, :, None, :], -1) * decay_in
    grad_end = grad_end + jnp.sum(in_term, 1)
    grad_ld = grad_ld - in_term
    end_mask = (local_pos == SPAN - 1).astype(jnp.float32)[None, :, None]
    grad_ld = grad_ld + end_mask * grad_end[:, None, :]
    grad_log = grad_ld.reshape(row_count, heads_here)
    grad_rate_sum = jnp.cumsum(grad_log[::-1], 0)[::-1]
    grad_inputs = grad_inputs_blocks.reshape(row_count, heads_here, head_size)
    grad_step = jnp.sum(grad_inputs * x_heads, -1) + grad_rate_sum * rates
    grad_a_log = jnp.sum(grad_rate_sum * step_size, 0) * rates
    grad_dt_in = grad_step * jax.nn.sigmoid(dt_in)
    grad_dt_bias = jnp.sum(grad_dt_in, 0)
    grad_x_heads = grad_y * d_skip[None, :, None] + grad_inputs * step_size[:, :, None]
    grad_bc = jnp.concatenate(
        [
            grad_b_blocks.reshape(row_count, state_width),
            grad_c_blocks.reshape(row_count, state_width),
        ],
        1,
    )
    grad_x_pre = grad_x_heads.reshape(row_count, width_here) * silu_grad(x_pre)
    grad_conv_x, grad_conv_x_bias, grad_proj_x = conv_back(proj_x, conv_x, conv_masks, grad_x_pre)
    grad_proj_low = grad_proj_x.astype(jnp.bfloat16)
    grad_w_x = jnp.dot(normed.T, grad_proj_low, preferred_element_type=jnp.float32)
    part_w_z = jnp.dot(normed.T, grad_z, preferred_element_type=jnp.float32)
    grad_w_z = dp_sum(part_w_z, n_dp, 1)
    grad_w_dt = jnp.dot(
        normed_wide.T, grad_dt_in, precision=highest, preferred_element_type=jnp.float32
    )
    grad_bc_pre = grad_bc * silu_grad(bc_pre)
    grad_conv_bc, grad_conv_bc_bias, grad_proj_bc = conv_back(
        proj_bc, conv_bc, conv_masks, grad_bc_pre
    )
    grad_bc_low = grad_proj_bc.astype(jnp.bfloat16)
    grad_w_bc = jnp.dot(normed.T, grad_bc_low, preferred_element_type=jnp.float32)
    low_all = jnp.concatenate(
        [grad_proj_low, grad_z, grad_bc_low, grad_dt_in.astype(jnp.bfloat16)], 1
    )
    w_all = jnp.concatenate([w_x, w_z, w_bc, w_dt], 1)

    def in_half(which):
        rows = lax.dynamic_slice_in_dim(low_all, which * half_rows, half_rows, 0)
        return jnp.dot(rows, w_all.T, preferred_element_type=jnp.float32)

    own_in, other_in, mine = wide_tensor_sum(in_half, n_tensor)
    grad_normed = join_halves(own_in, other_in, mine)
    weighted = grad_normed * norm_gain
    grad_norm_gain = (
        jnp.sum(grad_w_x * w_x.astype(jnp.float32), 1)
        + jnp.sum(part_w_z * w_z.astype(jnp.float32), 1)
        + jnp.sum(grad_w_dt * w_dt.astype(jnp.float32), 1)
        + jnp.sum(grad_w_bc * w_bc.astype(jnp.float32), 1)
    ) / norm_gain
    grad_hidden = (
        grad_out
        + inv_rms * weighted
        - hidden_wide * inv_rms**3 * jnp.mean(weighted * hidden_wide, -1, keepdims=True)
    )
    model_width = hidden.shape[1]
    bc_width = w_bc.shape[1]
    bc_parts = jnp.concatenate(
        [
            grad_w_bc,
            grad_conv_bc,
            grad_conv_bc_bias[None],
            grad_norm_gain.reshape(-1, bc_width),
        ],
        0,
    )
    bc_parts = pad_rows(bc_parts, 16 * n_dp)
    order = steps_of(n_dp)
    order = order[1:2] + order[:1] + order[2:]
    bc_parts = axis_scatter(bc_parts, "tensor", n_tensor, [1])
    bc_parts = axis_scatter(bc_parts, "dp", n_dp, order)
    for step in steps_of(n_tensor)[1:]:
        bc_parts = bc_parts + lax.ppermute(bc_parts, "tensor", partners(n_tensor, step))
    bc_parts = axis_gather(bc_parts, "dp", n_dp, order)
    bc_parts = axis_gather(bc_parts, "tensor", n_tensor, [1])
    conv_at = model_width + tap_count
    head_parts = jnp.stack([grad_dt_bias, grad_a_log, grad_d_skip], 0).reshape(1, -1)
    head_parts = jnp.pad(head_parts, ((0, 0), (0, width_here - head_parts.shape[1])))
    dt_parts = jnp.pad(grad_w_dt.T, ((0, 0), (0, -model_width % width_here)))
    x_parts = jnp.concatenate(
        [
            grad_w_x,
            grad_conv_x,
            grad_conv_x_bias[None],
            grad_gate_gain[None],
            head_parts,
            dt_parts.reshape(-1, width_here),
        ],
        0,
    )
    x_parts = dp_sum(pad_rows(x_parts, 8 * n_dp), n_dp, 0)
    at = model_width + tap_count
    heads_sum = x_parts[at + 2, : 3 * heads_here].reshape(3, heads_here)
    dt_rows = dt_parts.size // width_here
    dt_sum = x_parts[at + 3 : at + 3 + dt_rows].reshape(heads_here, -1)[:, :model_width].T
    norm_rows = model_width // bc_width
    return (
        output,
        grad_hidden,
        bc_parts[conv_at + 1 : conv_at + 1 + norm_rows].reshape(-1),
        x_parts[:model_width],
        grad_w_z,
        dt_sum,
        bc_parts[:model_width],
        x_parts[model_width:at],
        x_parts[at],
        bc_parts[model_width:conv_at],
        bc_parts[conv_at],
        heads_sum[0],
        heads_sum[1],
        heads_sum[2],
        x_parts[at + 1],
        grad_w_out,
    )


def solution(mesh):
    return jax.shard_map(
        functools.partial(per_device, mesh.shape["dp"], mesh.shape["tensor"]),
        mesh=mesh,
        in_specs=(
            P("dp", None),
            P("dp", None),
            P("dp"),
            P("dp"),
            P(),
            P(None, "tensor"),
            P(None, "tensor"),
            P(None, "tensor"),
            P(),
            P(None, "tensor"),
            P("tensor"),
            P(),
            P(),
            P("tensor"),
            P("tensor"),
            P("tensor"),
            P("tensor"),
            P("tensor", None),
        ),
        out_specs=(
            P("dp", None),
            P("dp", None),
            P(),
            P(None, "tensor"),
            P(None, "tensor"),
            P(None, "tensor"),
            P(),
            P(None, "tensor"),
            P("tensor"),
            P(),
            P(),
            P("tensor"),
            P("tensor"),
            P("tensor"),
            P("tensor"),
            P("tensor", None),
        ),
        check_vma=False,
    )
```

```python
import functools

import jax
import jax.numpy as jnp
from jax import lax
from jax.experimental import pallas as pl
from jax.experimental.pallas import tpu as pltpu
from jax.sharding import PartitionSpec as P

SPAN = 256
LANES = 128
EPS = 1e-05
FAR = -10000.0
FIRST = ((0,), (0,))
LAST = ((1,), (1,))


def dot(left, right, dims=((1,), (0,))):
    return lax.dot_general(left, right, (dims, ((), ())), preferred_element_type=jnp.float32)


def parts_of(values, count):
    parts = []
    for _ in range(count):
        part = values.astype(jnp.bfloat16)
        values = values - part.astype(jnp.float32)
        parts.append(part)
    return parts


def dot_left_exact(left, values, count):
    total = None
    for part in parts_of(values, count):
        product = dot(left, part)
        total = product if total is None else total + product
    return total


def dot_right_exact(values, right, dims):
    total = None
    for part in parts_of(values, 2):
        product = dot(part, right, dims)
        total = product if total is None else total + product
    return total


def sigmoid(values):
    return 1.0 / (1.0 + jnp.exp(-values))


def softplus(values):
    return jnp.maximum(values, 0.0) + jnp.log1p(jnp.exp(-jnp.abs(values)))


def lower_ones():
    down = lax.broadcasted_iota(jnp.int32, (SPAN, SPAN), 0)
    across = lax.broadcasted_iota(jnp.int32, (SPAN, SPAN), 1)
    return down >= across


def as_low(flags):
    return jnp.where(flags, 1.0, 0.0).astype(jnp.bfloat16)


def span_decays(dt_part, cols, seg_row, head_rows, spread, lower):
    dt_in = dt_part + head_rows[0:1]
    step = softplus(dt_in)
    falls = dot_left_exact(as_low(lower), step * head_rows[1:2], 3)
    falls_t = falls.T
    decay_in = jnp.exp(falls[SPAN - 1 : SPAN] - falls) * cols[:, 5:6]
    decay_out = jnp.exp(falls) * cols[:, 6:7]
    linked = lower & (cols[:, 0:1] == seg_row)
    wide = lambda values: dot_right_exact(values, spread, ((1,), (0,)))
    return dt_in, step, falls, falls_t, wide(step), wide(decay_in), wide(decay_out), linked


def fwd_kernel(
    hid_ref, cot_ref, cols_ref, seg_ref, gain_ref, wcat_ref, wout_ref, conv_ref, head_ref,
    spread_ref, chan_ref, normed_ref, conv_in_ref, z_ref, dt_ref, pre_ref, y_ref, gin_ref,
    carried_ref, sums_ref, ext_ref, state_ref, *, heads, inner, conv_width,
):
    @pl.when(pl.program_id(0) == 0)
    def _():
        ext_ref[0:8, :] = jnp.zeros((8, conv_width), jnp.float32)
        state_ref[...] = jnp.zeros_like(state_ref)

    cols = cols_ref[...]
    hid = hid_ref[...].astype(jnp.float32)
    inv_rms = lax.rsqrt(jnp.mean(hid * hid, -1, keepdims=True) + EPS)
    normed = (hid * inv_rms * gain_ref[...]).astype(jnp.bfloat16)
    normed_ref[...] = normed
    conv_in = dot(normed, wcat_ref[:, 0:conv_width])
    gate_in = dot(normed, wcat_ref[:, conv_width : conv_width + inner])
    dt_part = dot(normed, wcat_ref[:, conv_width + inner :])
    conv_in_ref[...] = conv_in
    z_ref[...] = gate_in
    dt_ref[...] = dt_part
    ext_ref[8 : 8 + SPAN, :] = conv_in
    pre = conv_ref[4:5] + conv_ref[0:1] * conv_in
    for lag in range(1, 4):
        earlier = ext_ref[8 - lag : 8 - lag + SPAN, :]
        pre = pre + conv_ref[lag : lag + 1] * (earlier * cols[:, lag : lag + 1])
    ext_ref[0:8, :] = conv_in[SPAN - 8 :]
    pre_ref[...] = pre
    active = pre * sigmoid(pre)
    x_conv = active[:, :inner]
    states = (conv_width - inner) // 2
    b_low = active[:, inner : inner + states].astype(jnp.bfloat16)
    c_low = active[:, inner + states :].astype(jnp.bfloat16)
    lower = lower_ones()
    _, _, falls, falls_t, step_x, in_x, out_x, linked = span_decays(
        dt_part, cols, seg_ref[0], head_ref[...], spread_ref[...], lower
    )
    kernel = dot(c_low, b_low, LAST)
    inputs = (step_x * x_conv).astype(jnp.bfloat16)
    size = inner // heads
    group = LANES // size
    lane_head = lax.broadcasted_iota(jnp.int32, (SPAN, LANES), 1) // size
    local = []
    for first in range(0, heads, group):
        at = first * size
        total = None
        for head in range(first, first + group):
            decay = jnp.exp(
                jnp.where(linked, falls[:, head : head + 1] - falls_t[head : head + 1, :], FAR)
            )
            mixing = (kernel * decay).astype(jnp.bfloat16)
            own = jnp.where(lane_head == head - first, inputs[:, at : at + LANES], 0)
            part = dot(mixing, own.astype(jnp.bfloat16))
            total = part if total is None else total + part
        local.append(total)
    local = jnp.concatenate(local, 1)
    carried = state_ref[...].astype(jnp.bfloat16)
    carried_ref[0] = carried
    y_flat = local + out_x * dot(c_low, carried) + chan_ref[0:1] * x_conv
    entering = (inputs.astype(jnp.float32) * in_x).astype(jnp.bfloat16)
    state_ref[...] = out_x[SPAN - 1 : SPAN] * state_ref[...] + dot(b_low, entering, FIRST)
    y_ref[...] = y_flat
    gated = y_flat * (gate_in * sigmoid(gate_in))
    grad_mix = (cols[:, 4:5] * cot_ref[...].astype(jnp.float32)).astype(jnp.bfloat16)
    grad_in = dot(grad_mix, wout_ref[...], LAST)
    gin_ref[...] = grad_in
    squares = jnp.sum(gated * gated, -1, keepdims=True)
    cross = jnp.sum(grad_in * chan_ref[1:2] * gated, -1, keepdims=True)
    lane = lax.broadcasted_iota(jnp.int32, (SPAN, LANES), 1)
    sums_ref[0] = jnp.where(lane == 0, squares, cross).T[0:2]


def gate_kernel(
    shift_ref, sums_ref, z_ref, y_ref, gin_ref, cot_ref, cols_ref, normed_ref, wout_ref, chan_ref,
    sent_ref, kept_ref, gy_ref, gz_ref, weights_ref, gain_ref, *, inner, inner_all,
):
    index = pl.program_id(0)
    half = pl.num_programs(0) // 2

    @pl.when(index == 0)
    def _():
        weights_ref[...] = jnp.zeros_like(weights_ref)
        gain_ref[...] = jnp.zeros_like(gain_ref)

    sums = sums_ref[0]
    copies = inner // LANES
    over = lambda row: jnp.concatenate([jnp.broadcast_to(row, (LANES, SPAN)).T] * copies, 1)
    squares, cross = over(sums[0:1]), over(sums[1:2])
    inv_gate = lax.rsqrt(squares / inner_all + EPS)
    gate_in = z_ref[...]
    y_flat = y_ref[...]
    sig = sigmoid(gate_in)
    active = gate_in * sig
    gated = y_flat * active
    scaled = gated * inv_gate
    out_in = (scaled * chan_ref[1:2]).astype(jnp.bfloat16)
    mixed = dot(out_in, wout_ref[...])

    @pl.when(index < half)
    def _():
        sent_ref[...] = mixed

    @pl.when(index >= half)
    def _():
        kept_ref[...] = mixed

    grad_mix = (cols_ref[:, 4:5] * cot_ref[...].astype(jnp.float32)).astype(jnp.bfloat16)
    weights_ref[0:inner, :] += dot(out_in, grad_mix, FIRST)
    grad_in = gin_ref[...]
    gain_ref[0:1, :] += jnp.sum(grad_in * scaled, 0, keepdims=True)
    grad_gated = inv_gate * (
        grad_in * chan_ref[1:2] - scaled * inv_gate * (cross * (1.0 / inner_all))
    )
    gy_ref[...] = grad_gated * active
    grad_z = (grad_gated * y_flat * (sig * (1.0 + gate_in * (1.0 - sig)))).astype(jnp.bfloat16)
    gz_ref[...] = grad_z
    weights_ref[inner : 2 * inner, :] += dot(grad_z, normed_ref[...], FIRST)


def bwd_kernel(
    shift_ref, cols_ref, seg_ref, normed_ref, conv_in_ref, dt_ref, pre_ref, y_ref, gy_ref, gz_ref,
    carried_ref, wcat_ref, conv_ref, head_ref, spread_ref, chan_ref,
    sent_ref, kept_ref, weights_ref, conv_grad_ref, head_grad_ref, ext_ref, flow_ref,
    *, heads, inner, conv_width,
):
    index = pl.program_id(0)
    half = pl.num_programs(0) // 2

    @pl.when(index == 0)
    def _():
        weights_ref[...] = jnp.zeros_like(weights_ref)
        conv_grad_ref[...] = jnp.zeros_like(conv_grad_ref)
        head_grad_ref[...] = jnp.zeros_like(head_grad_ref)

    @pl.when((index == 0) | (index == half))
    def _():
        ext_ref[SPAN : SPAN + 8, :] = jnp.zeros((8, conv_width), jnp.float32)
        flow_ref[...] = jnp.zeros_like(flow_ref)

    cols = cols_ref[...]
    pre = pre_ref[...]
    sig = sigmoid(pre)
    active = pre * sig
    slope = sig * (1.0 + pre * (1.0 - sig))
    x_conv = active[:, :inner]
    states = (conv_width - inner) // 2
    b_low = active[:, inner : inner + states].astype(jnp.bfloat16)
    c_low = active[:, inner + states :].astype(jnp.bfloat16)
    lower = lower_ones()
    spread = spread_ref[...]
    head_rows = head_ref[...]
    dt_in, step, falls, falls_t, step_x, in_x, out_x, linked = span_decays(
        dt_ref[...], cols, seg_ref[0], head_rows, spread, lower
    )
    kernel = dot(c_low, b_low, LAST)
    inputs = (step_x * x_conv).astype(jnp.bfloat16)
    grad_y = gy_ref[...]
    grad_scan = grad_y.astype(jnp.bfloat16)
    size = inner // heads
    group = LANES // size
    lane_head = lax.broadcasted_iota(jnp.int32, (SPAN, LANES), 1) // size
    grad_kernel = None
    grad_inputs = []
    for first in range(0, heads, group):
        at = first * size
        total = None
        for head in range(first, first + group):
            decay = jnp.exp(
                jnp.where(linked, falls[:, head : head + 1] - falls_t[head : head + 1, :], FAR)
            )
            mixing = (kernel * decay).astype(jnp.bfloat16)
            here = lane_head == head - first
            own = jnp.where(here, grad_scan[:, at : at + LANES], 0).astype(jnp.bfloat16)
            grad_part = dot(own, inputs[:, at : at + LANES], LAST) * decay
            grad_kernel = grad_part if grad_kernel is None else grad_kernel + grad_part
            part = dot(mixing, own, FIRST)
            total = part if total is None else total + part
        grad_inputs.append(total)
    flow = flow_ref[...]
    flow_low = flow.astype(jnp.bfloat16)
    grad_inputs = jnp.concatenate(grad_inputs, 1) + in_x * dot(b_low, flow_low)
    grad_kernel = grad_kernel.astype(jnp.bfloat16)
    inputs_wide = inputs.astype(jnp.float32)
    leaving, leaving_rest = parts_of(out_x * grad_scan.astype(jnp.float32), 2)
    entering = (in_x * inputs_wide).astype(jnp.bfloat16)
    grad_c = dot(grad_kernel, b_low) + dot(leaving, carried_ref[0], LAST)
    grad_b = dot(grad_kernel, c_low, FIRST) + dot(entering, flow_low, LAST)
    grad_carried = dot(c_low, leaving, FIRST) + dot(c_low, leaving_rest, FIRST)
    flow = out_x[SPAN - 1 : SPAN] * flow + grad_carried
    flow_ref[...] = flow
    crossing = jnp.sum(flow * carried_ref[0].astype(jnp.float32), 0, keepdims=True)
    crossing = dot_right_exact(jnp.broadcast_to(crossing, (8, inner)), spread, LAST)
    scanned = y_ref[...] - chan_ref[0:1] * x_conv
    grad_log = dot_right_exact(
        grad_scan.astype(jnp.float32) * scanned - inputs_wide * grad_inputs, spread, LAST
    )
    earlier = as_low(jnp.logical_not(upper_ones()))
    rate_sum = crossing[0:1] - dot_left_exact(earlier, grad_log, 3)
    grad_step = dot_right_exact(grad_inputs * x_conv, spread, LAST) + rate_sum * head_rows[1:2]
    grad_dt = grad_step * sigmoid(dt_in)
    head_grad_ref[0:1, :] += jnp.sum(grad_dt, 0, keepdims=True)
    head_grad_ref[1:2, :] += jnp.sum(rate_sum * step, 0, keepdims=True) * head_rows[1:2]
    grad_x = grad_y * chan_ref[0:1] + grad_inputs * step_x
    conv_grad_ref[5:6, 0:inner] += jnp.sum(grad_y * x_conv, 0, keepdims=True)
    grad_pre = jnp.concatenate([grad_x, grad_b, grad_c], 1) * slope
    conv_in = conv_in_ref[...]
    ext_ref[0:SPAN, :] = grad_pre
    grad_conv_in = conv_ref[0:1] * grad_pre
    conv_grad_ref[0:1, :] += jnp.sum(grad_pre * conv_in, 0, keepdims=True)
    conv_grad_ref[4:5, :] += jnp.sum(grad_pre, 0, keepdims=True)
    for lag in range(1, 4):
        term = ext_ref[lag : lag + SPAN, :] * cols[:, 7 + lag : 8 + lag]
        grad_conv_in = grad_conv_in + conv_ref[lag : lag + 1] * term
        conv_grad_ref[lag : lag + 1, :] += jnp.sum(term * conv_in, 0, keepdims=True)
    ext_ref[SPAN : SPAN + 8, :] = grad_pre[0:8]
    conv_low = grad_conv_in.astype(jnp.bfloat16)
    dt_low = grad_dt.astype(jnp.bfloat16)
    low = jnp.concatenate([conv_low, gz_ref[...], dt_low], 1)
    partial = dot(low, wcat_ref[...], LAST)

    @pl.when(index < half)
    def _():
        sent_ref[...] = partial

    @pl.when(index >= half)
    def _():
        kept_ref[...] = partial

    normed = normed_ref[...]
    weights_ref[0:conv_width, :] += dot(conv_low, normed, FIRST)
    weights_ref[conv_width:, :] += dot(dt_low, normed, FIRST)


def upper_ones():
    down = lax.broadcasted_iota(jnp.int32, (SPAN, SPAN), 0)
    across = lax.broadcasted_iota(jnp.int32, (SPAN, SPAN), 1)
    return down <= across


def finish_kernel(place_ref, own_ref, other_ref, hid_ref, cot_ref, gain_ref, out_ref):
    half = pl.num_programs(0) // 2
    mine = pl.program_id(0) // half == place_ref[0]
    hid = hid_ref[...].astype(jnp.float32)
    inv_rms = lax.rsqrt(jnp.mean(hid * hid, -1, keepdims=True) + EPS)

    def write(values):
        weighted = values * gain_ref[...]
        inner = jnp.mean(weighted * hid, -1, keepdims=True)
        out_ref[...] = (
            cot_ref[...].astype(jnp.float32)
            + inv_rms * weighted
            - hid * (inv_rms * inv_rms * inv_rms * inner)
        )

    @pl.when(mine)
    def _():
        write(own_ref[...])

    @pl.when(jnp.logical_not(mine))
    def _():
        write(other_ref[...])


def partners(count, step):
    return [(place, place ^ step) for place in range(count)]


def steps_of(count):
    return [1 << level for level in range((count - 1).bit_length())]


def take_half(values, which):
    half = values.shape[0] // 2
    return lax.dynamic_slice_in_dim(values, which * half, half, 0)


def join_halves(own, other, mine):
    return jnp.where(
        mine == 0, jnp.concatenate([own, other], 0), jnp.concatenate([other, own], 0)
    )


def axis_scatter(values, axis, count, order):
    place = lax.axis_index(axis)
    for step in order:
        mine = (place // step) % 2
        sent = lax.ppermute(take_half(values, 1 - mine), axis, partners(count, step))
        values = take_half(values, mine) + sent
    return values


def axis_gather(values, axis, count, order):
    place = lax.axis_index(axis)
    for step in reversed(order):
        other = lax.ppermute(values, axis, partners(count, step))
        values = join_halves(values, other, (place // step) % 2)
    return values


def dp_sum(values, count, first):
    order = steps_of(count)
    order = order[first:2] + order[:first] + order[2:]
    return axis_gather(axis_scatter(values, "dp", count, order), "dp", count, order)


def wide_tensor_sum(sent, kept, count):
    values = kept + lax.ppermute(sent, "tensor", partners(count, 1))
    for step in steps_of(count)[1:]:
        values = values + lax.ppermute(values, "tensor", partners(count, step))
    return values, lax.ppermute(values, "tensor", partners(count, 1))


def pad_rows(values, multiple):
    return jnp.pad(values, ((0, -values.shape[0] % multiple), (0, 0)))


def call(kernel, grid, prefetch, ins, in_specs, outs, out_specs, scratch, flops):
    moved = sum(a.size * a.dtype.itemsize for a in ins) + sum(
        o.size * o.dtype.itemsize for o in outs
    )
    return pl.pallas_call(
        kernel,
        grid_spec=pltpu.PrefetchScalarGridSpec(
            num_scalar_prefetch=len(prefetch),
            grid=grid,
            in_specs=in_specs,
            out_specs=out_specs,
            scratch_shapes=scratch,
        ),
        out_shape=outs,
        cost_estimate=pl.CostEstimate(flops=flops, bytes_accessed=moved, transcendentals=0),
    )(*prefetch, *ins)


def per_device(
    n_dp,
    n_tensor,
    hidden,
    cotangent,
    seg_ids,
    counts,
    norm_gain,
    w_x,
    w_z,
    w_dt,
    w_bc,
    conv_x,
    conv_x_bias,
    conv_bc,
    conv_bc_bias,
    dt_bias,
    a_log,
    d_skip,
    gate_gain,
    w_out,
):
    f32, bf16 = jnp.float32, jnp.bfloat16
    rows, width = hidden.shape
    bc_width = w_bc.shape[1]
    states = bc_width // 2
    heads = w_dt.shape[1]
    inner = w_x.shape[1]
    taps = conv_x.shape[0]
    size = inner // heads
    spans = rows // SPAN
    half_spans = spans // 2
    conv_width = inner + bc_width
    all_width = conv_width + inner + LANES
    mine = lax.axis_index("tensor") % 2
    positions = jnp.arange(rows)
    seg_spans = seg_ids.reshape(spans, SPAN)
    seg_end = seg_spans[:, -1:]
    seg_prev = jnp.concatenate([jnp.full((1, 1), -1, jnp.int32), seg_end[:-1]], 0)

    def conv_link(lag):
        ahead = jnp.concatenate([jnp.full((lag,), -1, jnp.int32), seg_ids[:-lag]])
        return ahead == seg_ids

    def conv_link_next(lag):
        behind = jnp.concatenate([seg_ids[lag:], jnp.full((lag,), -1, jnp.int32)])
        return behind == seg_ids

    cols = jnp.stack(
        [
            seg_ids.astype(f32),
            conv_link(1).astype(f32),
            conv_link(2).astype(f32),
            conv_link(3).astype(f32),
            (positions < counts[0]).astype(f32),
            (seg_spans == seg_end).reshape(rows).astype(f32),
            (seg_spans == seg_prev).reshape(rows).astype(f32),
            jnp.zeros((rows,), f32),
            conv_link_next(1).astype(f32),
            conv_link_next(2).astype(f32),
            conv_link_next(3).astype(f32),
        ],
        1,
    )
    cols = jnp.pad(cols, ((0, 0), (0, 16 - cols.shape[1])))
    seg_rows = seg_spans.astype(f32)[:, None, :]
    w_cat = jnp.concatenate([w_x, w_bc, w_z, jnp.pad(w_dt, ((0, 0), (0, LANES - heads)))], 1)
    conv_rows = jnp.concatenate(
        [
            jnp.concatenate([conv_x, conv_bc], 1),
            jnp.concatenate([conv_x_bias, conv_bc_bias])[None],
        ],
        0,
    )
    conv_rows = jnp.pad(conv_rows, ((0, 8 - conv_rows.shape[0]), (0, 0)))
    head_rows = jnp.pad(
        jnp.stack([dt_bias, -jnp.exp(a_log)], 0), ((0, 6), (0, LANES - heads))
    )
    spread = (jnp.arange(LANES)[:, None] == jnp.arange(inner)[None, :] // size).astype(bf16)
    chan = jnp.pad(jnp.stack([jnp.repeat(d_skip, size), gate_gain], 0), ((0, 6), (0, 0)))
    gain = norm_gain[None]

    def shape(*dims, dtype=f32):
        return jax.ShapeDtypeStruct(dims, dtype)

    def whole(array):
        return pl.BlockSpec(array.shape, lambda *_: (0,) * len(array.shape))

    def plain(columns):
        return pl.BlockSpec((SPAN, columns), lambda i: (i, 0))

    normed, conv_in, gate_in, dt_part, pre, y_flat, grad_in, carried, sums = call(
        functools.partial(fwd_kernel, heads=heads, inner=inner, conv_width=conv_width),
        (spans,),
        (),
        (hidden, cotangent, cols, seg_rows, gain, w_cat, w_out, conv_rows, head_rows, spread, chan),
        [plain(width), plain(width), plain(16), pl.BlockSpec((1, 1, SPAN), lambda i: (i, 0, 0))]
        + [whole(a) for a in (gain, w_cat, w_out, conv_rows, head_rows, spread, chan)],
        (
            shape(rows, width, dtype=bf16),
            shape(rows, conv_width),
            shape(rows, inner),
            shape(rows, LANES),
            shape(rows, conv_width),
            shape(rows, inner),
            shape(rows, inner),
            shape(spans, states, inner, dtype=bf16),
            shape(spans, 2, SPAN),
        ),
        [
            plain(width), plain(conv_width), plain(inner), plain(LANES), plain(conv_width),
            plain(inner), plain(inner),
            pl.BlockSpec((1, states, inner), lambda i: (i, 0, 0)),
            pl.BlockSpec((1, 2, SPAN), lambda i: (i, 0, 0)),
        ],
        [pltpu.VMEM((SPAN + 8, conv_width), f32), pltpu.VMEM((states, inner), f32)],
        2 * rows * (width * (all_width + inner) + heads * SPAN * LANES),
    )
    for step in steps_of(n_tensor):
        sums = sums + lax.ppermute(sums, "tensor", partners(n_tensor, step))
    shift = (half_spans * (1 - mine)).astype(jnp.int32).reshape(1)

    def turned(columns):
        return pl.BlockSpec((SPAN, columns), lambda i, s: ((i + s[0]) % spans, 0))

    sent_spec = pl.BlockSpec((SPAN, width), lambda i, s: (jnp.minimum(i, half_spans - 1), 0))
    kept_spec = pl.BlockSpec((SPAN, width), lambda i, s: (jnp.maximum(i - half_spans, 0), 0))
    mixed_sent, mixed_kept, grad_y, grad_z, early, gate_grad = call(
        functools.partial(gate_kernel, inner=inner, inner_all=inner * n_tensor),
        (spans,),
        (shift,),
        (sums, gate_in, y_flat, grad_in, cotangent, cols, normed, w_out, chan),
        [
            pl.BlockSpec((1, 2, SPAN), lambda i, s: ((i + s[0]) % spans, 0, 0)),
            turned(inner), turned(inner), turned(inner), turned(width), turned(16),
            turned(width), whole(w_out), whole(chan),
        ],
        (
            shape(rows // 2, width),
            shape(rows // 2, width),
            shape(rows, inner),
            shape(rows, inner, dtype=bf16),
            shape(2 * inner, width),
            shape(8, inner),
        ),
        [
            sent_spec, kept_spec, turned(inner), turned(inner),
            pl.BlockSpec((2 * inner, width), lambda i, s: (0, 0)),
            pl.BlockSpec((8, inner), lambda i, s: (0, 0)),
        ],
        [],
        2 * rows * width * inner * 3,
    )
    mixed_own, mixed_other = wide_tensor_sum(mixed_sent, mixed_kept, n_tensor)
    early_sum = dp_sum(early, n_dp, 0)

    def back_at(i, s):
        turn = i // half_spans
        return ((turn + s[0] // half_spans) % 2) * half_spans + half_spans - 1 - i % half_spans

    def back(columns):
        return pl.BlockSpec((SPAN, columns), lambda i, s: (back_at(i, s), 0))

    def low_at(i):
        return half_spans - 1 - i % half_spans

    partial_sent, partial_kept, late, conv_grad, head_grad = call(
        functools.partial(bwd_kernel, heads=heads, inner=inner, conv_width=conv_width),
        (spans,),
        (shift,),
        (
            cols, seg_rows, normed, conv_in, dt_part, pre, y_flat, grad_y, grad_z, carried, w_cat,
            conv_rows, head_rows, spread, chan,
        ),
        [
            back(16), pl.BlockSpec((1, 1, SPAN), lambda i, s: (back_at(i, s), 0, 0)),
            back(width), back(conv_width), back(LANES), back(conv_width), back(inner),
            back(inner), back(inner),
            pl.BlockSpec((1, states, inner), lambda i, s: (back_at(i, s), 0, 0)),
        ]
        + [whole(a) for a in (w_cat, conv_rows, head_rows, spread, chan)],
        (
            shape(rows // 2, width),
            shape(rows // 2, width),
            shape(conv_width + LANES, width),
            shape(8, conv_width),
            shape(8, LANES),
        ),
        [
            pl.BlockSpec((SPAN, width), lambda i, s: (jnp.where(i < half_spans, low_at(i), 0), 0)),
            pl.BlockSpec(
                (SPAN, width),
                lambda i, s: (jnp.where(i < half_spans, half_spans - 1, low_at(i)), 0),
            ),
            pl.BlockSpec((conv_width + LANES, width), lambda i, s: (0, 0)),
            pl.BlockSpec((8, conv_width), lambda i, s: (0, 0)),
            pl.BlockSpec((8, LANES), lambda i, s: (0, 0)),
        ],
        [
            pltpu.VMEM((SPAN + 8, conv_width), f32),
            pltpu.VMEM((states, inner), f32),
        ],
        2 * rows * (width * all_width * 2 + heads * SPAN * LANES * 2),
    )
    normed_own, normed_other = wide_tensor_sum(partial_sent, partial_kept, n_tensor)
    w_wide = w_cat.T.astype(f32)
    norm_grad = (
        jnp.sum(late[:conv_width] * w_wide[:conv_width], 0)
        + jnp.sum(late[conv_width:] * w_wide[conv_width + inner :], 0)
        + jnp.sum(early[inner:] * w_wide[conv_width : conv_width + inner], 0)
    ) / norm_gain

    def widen(values):
        flat = values.reshape(-1)
        return jnp.pad(flat, (0, -flat.size % width)).reshape(-1, width)

    bc_small = jnp.concatenate([conv_grad[:5, inner:].reshape(-1), norm_grad])
    bc_parts = pad_rows(
        jnp.concatenate([late[inner:conv_width], widen(bc_small)], 0), 16 * n_dp
    )
    order = steps_of(n_dp)
    order = order[1:2] + order[:1] + order[2:]
    bc_parts = axis_scatter(bc_parts, "tensor", n_tensor, [1])
    bc_parts = axis_scatter(bc_parts, "dp", n_dp, order)
    for step in steps_of(n_tensor)[1:]:
        bc_parts = bc_parts + lax.ppermute(bc_parts, "tensor", partners(n_tensor, step))
    bc_parts = axis_gather(bc_parts, "dp", n_dp, order)
    bc_parts = axis_gather(bc_parts, "tensor", n_tensor, [1])
    x_small = jnp.concatenate(
        [
            conv_grad[:5, :inner].reshape(-1),
            gate_grad[0],
            head_grad[0, :heads],
            head_grad[1, :heads],
            jnp.sum(conv_grad[5, :inner].reshape(heads, size), 1),
        ]
    )
    x_parts = pad_rows(
        jnp.concatenate(
            [late[:inner], late[conv_width : conv_width + heads], widen(x_small)], 0
        ),
        8 * n_dp,
    )
    x_parts = dp_sum(x_parts, n_dp, 0)
    x_small = x_parts[inner + heads :].reshape(-1)
    bc_small = bc_parts[bc_width:].reshape(-1)
    at = (taps + 1) * inner
    bc_at = (taps + 1) * bc_width
    mixed = join_halves(mixed_own, mixed_other, mine)
    output = (hidden.astype(f32) + cols[:, 4:5] * mixed).astype(bf16)
    place = mine.astype(jnp.int32).reshape(1)
    half_spec = pl.BlockSpec((SPAN, width), lambda i, s: (i % half_spans, 0))
    row_spec = pl.BlockSpec((SPAN, width), lambda i, s: (i, 0))
    (grad_hidden,) = call(
        finish_kernel,
        (spans,),
        (place,),
        (normed_own, normed_other, hidden, cotangent, gain),
        [half_spec, half_spec, row_spec, row_spec, whole(gain)],
        (shape(rows, width),),
        [row_spec],
        [],
        rows * width * 10,
    )
    return (
        output,
        grad_hidden,
        bc_small[bc_at : bc_at + width],
        x_parts[:inner].T,
        early_sum[inner:].T,
        x_parts[inner : inner + heads].T,
        bc_parts[:bc_width].T,
        x_small[: taps * inner].reshape(taps, inner),
        x_small[taps * inner : at],
        bc_small[: taps * bc_width].reshape(taps, bc_width),
        bc_small[taps * bc_width : bc_at],
        x_small[at + inner : at + inner + heads],
        x_small[at + inner + heads : at + inner + 2 * heads],
        x_small[at + inner + 2 * heads : at + inner + 3 * heads],
        x_small[at : at + inner],
        early_sum[:inner],
    )


def solution(mesh):
    return jax.shard_map(
        functools.partial(per_device, mesh.shape["dp"], mesh.shape["tensor"]),
        mesh=mesh,
        in_specs=(
            P("dp", None),
            P("dp", None),
            P("dp"),
            P("dp"),
            P(),
            P(None, "tensor"),
            P(None, "tensor"),
            P(None, "tensor"),
            P(),
            P(None, "tensor"),
            P("tensor"),
            P(),
            P(),
            P("tensor"),
            P("tensor"),
            P("tensor"),
            P("tensor"),
            P("tensor", None),
        ),
        out_specs=(
            P("dp", None),
            P("dp", None),
            P(),
            P(None, "tensor"),
            P(None, "tensor"),
            P(None, "tensor"),
            P(),
            P(None, "tensor"),
            P("tensor"),
            P(),
            P(),
            P("tensor"),
            P("tensor"),
            P("tensor"),
            P("tensor"),
            P("tensor", None),
        ),
        check_vma=False,
    )
```

```python
import functools

import jax
import jax.numpy as jnp
from jax import lax
from jax.experimental import pallas as pl
from jax.experimental.pallas import tpu as pltpu
from jax.sharding import PartitionSpec as P

SPAN = 256
LANES = 128
EPS = 1e-05
FAR = -10000.0
FIRST = ((0,), (0,))
LAST = ((1,), (1,))


def dot(left, right, dims=((1,), (0,))):
    return lax.dot_general(left, right, (dims, ((), ())), preferred_element_type=jnp.float32)


def parts_of(values, count):
    parts = []
    for _ in range(count):
        part = values.astype(jnp.bfloat16)
        values = values - part.astype(jnp.float32)
        parts.append(part)
    return parts


def dot_left_exact(left, values, count):
    total = None
    for part in parts_of(values, count):
        product = dot(left, part)
        total = product if total is None else total + product
    return total


def dot_right_exact(values, right, dims):
    total = None
    for part in parts_of(values, 2):
        product = dot(part, right, dims)
        total = product if total is None else total + product
    return total


def sigmoid(values):
    return 1.0 / (1.0 + jnp.exp(-values))


def softplus(values):
    return jnp.maximum(values, 0.0) + jnp.log1p(jnp.exp(-jnp.abs(values)))


def lower_ones():
    down = lax.broadcasted_iota(jnp.int32, (SPAN, SPAN), 0)
    across = lax.broadcasted_iota(jnp.int32, (SPAN, SPAN), 1)
    return down >= across


def as_low(flags):
    return jnp.where(flags, 1.0, 0.0).astype(jnp.bfloat16)


def span_decays(dt_part, cols, seg_row, head_rows, spread, lower):
    dt_in = dt_part + head_rows[0:1]
    step = softplus(dt_in)
    falls = dot_left_exact(as_low(lower), step * head_rows[1:2], 3)
    falls_t = falls.T
    decay_in = jnp.exp(falls[SPAN - 1 : SPAN] - falls) * cols[:, 5:6]
    decay_out = jnp.exp(falls) * cols[:, 6:7]
    linked = lower & (cols[:, 0:1] == seg_row)
    wide = lambda values: dot_right_exact(values, spread, ((1,), (0,)))
    return dt_in, step, falls, falls_t, wide(step), wide(decay_in), wide(decay_out), linked


def fwd_kernel(
    hid_ref, cot_ref, cols_ref, seg_ref, gain_ref, wcat_ref, wout_ref, conv_ref, head_ref,
    spread_ref, chan_ref, normed_ref, conv_in_ref, z_ref, dt_ref, pre_ref, y_ref, gin_ref,
    carried_ref, sums_ref, ext_ref, state_ref, *, heads, inner, conv_width,
):
    @pl.when(pl.program_id(0) == 0)
    def _():
        ext_ref[0:8, :] = jnp.zeros((8, conv_width), jnp.float32)
        state_ref[...] = jnp.zeros_like(state_ref)

    cols = cols_ref[...]
    hid = hid_ref[...].astype(jnp.float32)
    inv_rms = lax.rsqrt(jnp.mean(hid * hid, -1, keepdims=True) + EPS)
    normed = (hid * inv_rms * gain_ref[...]).astype(jnp.bfloat16)
    normed_ref[...] = normed
    conv_in = dot(normed, wcat_ref[:, 0:conv_width])
    gate_in = dot(normed, wcat_ref[:, conv_width : conv_width + inner])
    dt_part = dot(normed, wcat_ref[:, conv_width + inner :])
    conv_in_ref[...] = conv_in
    z_ref[...] = gate_in
    dt_ref[...] = dt_part
    ext_ref[8 : 8 + SPAN, :] = conv_in
    pre = conv_ref[4:5] + conv_ref[0:1] * conv_in
    for lag in range(1, 4):
        earlier = ext_ref[8 - lag : 8 - lag + SPAN, :]
        pre = pre + conv_ref[lag : lag + 1] * (earlier * cols[:, lag : lag + 1])
    ext_ref[0:8, :] = conv_in[SPAN - 8 :]
    pre_ref[...] = pre
    active = pre * sigmoid(pre)
    x_conv = active[:, :inner]
    states = (conv_width - inner) // 2
    b_low = active[:, inner : inner + states].astype(jnp.bfloat16)
    c_low = active[:, inner + states :].astype(jnp.bfloat16)
    lower = lower_ones()
    _, _, falls, falls_t, step_x, in_x, out_x, linked = span_decays(
        dt_part, cols, seg_ref[0], head_ref[...], spread_ref[...], lower
    )
    kernel = dot(c_low, b_low, LAST)
    inputs = (step_x * x_conv).astype(jnp.bfloat16)
    size = inner // heads
    group = LANES // size
    lane_head = lax.broadcasted_iota(jnp.int32, (SPAN, LANES), 1) // size
    local = []
    for first in range(0, heads, group):
        at = first * size
        total = None
        for head in range(first, first + group):
            decay = jnp.exp(
                jnp.where(linked, falls[:, head : head + 1] - falls_t[head : head + 1, :], FAR)
            )
            mixing = (kernel * decay).astype(jnp.bfloat16)
            own = jnp.where(lane_head == head - first, inputs[:, at : at + LANES], 0)
            part = dot(mixing, own.astype(jnp.bfloat16))
            total = part if total is None else total + part
        local.append(total)
    local = jnp.concatenate(local, 1)
    carried = state_ref[...].astype(jnp.bfloat16)
    carried_ref[0] = carried
    y_flat = local + out_x * dot(c_low, carried) + chan_ref[0:1] * x_conv
    entering = (inputs.astype(jnp.float32) * in_x).astype(jnp.bfloat16)
    state_ref[...] = out_x[SPAN - 1 : SPAN] * state_ref[...] + dot(b_low, entering, FIRST)
    y_ref[...] = y_flat
    gated = y_flat * (gate_in * sigmoid(gate_in))
    grad_mix = (cols[:, 4:5] * cot_ref[...].astype(jnp.float32)).astype(jnp.bfloat16)
    grad_in = dot(grad_mix, wout_ref[...], LAST)
    gin_ref[...] = grad_in
    squares = jnp.sum(gated * gated, -1, keepdims=True)
    cross = jnp.sum(grad_in * chan_ref[1:2] * gated, -1, keepdims=True)
    lane = lax.broadcasted_iota(jnp.int32, (SPAN, LANES), 1)
    sums_ref[0] = jnp.where(lane == 0, squares, cross).T[0:2]


def split_refs(refs, count):
    return (refs[:count], refs[count:]) if len(refs) > 7 else ((), refs)


def begin_sums(targets, sources):
    @pl.when(pl.program_id(0) == 0)
    def _():
        for place, target in enumerate(targets):
            target[...] = sources[place][...] if sources else jnp.zeros_like(target)


def store_halves(place_ref, values, sent_ref, kept_ref):
    half = values.shape[1] // 2

    @pl.when(place_ref[0] == 0)
    def _():
        kept_ref[...] = values[:, :half]
        sent_ref[...] = values[:, half:]

    @pl.when(place_ref[0] == 1)
    def _():
        kept_ref[...] = values[:, half:]
        sent_ref[...] = values[:, :half]


def join_columns(place_ref, own_ref, other_ref, write):
    own, other = own_ref[...], other_ref[...]

    @pl.when(place_ref[0] == 0)
    def _():
        write(jnp.concatenate([own, other], 1))

    @pl.when(place_ref[0] == 1)
    def _():
        write(jnp.concatenate([other, own], 1))


def gate_kernel(
    place_ref, sums_ref, z_ref, y_ref, gin_ref, cot_ref, cols_ref, normed_ref, wout_ref, chan_ref,
    *refs, inner, inner_all,
):
    sums_of, outs = split_refs(refs, 3)
    sent_ref, kept_ref, gy_ref, gz_ref, wout_grad_ref, wz_grad_ref, gain_ref = outs
    begin_sums((wout_grad_ref, wz_grad_ref, gain_ref), sums_of)

    sums = sums_ref[0]
    copies = inner // LANES
    over = lambda row: jnp.concatenate([jnp.broadcast_to(row, (LANES, SPAN)).T] * copies, 1)
    squares, cross = over(sums[0:1]), over(sums[1:2])
    inv_gate = lax.rsqrt(squares / inner_all + EPS)
    gate_in = z_ref[...]
    y_flat = y_ref[...]
    sig = sigmoid(gate_in)
    active = gate_in * sig
    gated = y_flat * active
    scaled = gated * inv_gate
    out_in = (scaled * chan_ref[1:2]).astype(jnp.bfloat16)
    store_halves(place_ref, dot(out_in, wout_ref[...]), sent_ref, kept_ref)
    grad_mix = (cols_ref[:, 4:5] * cot_ref[...].astype(jnp.float32)).astype(jnp.bfloat16)
    wout_grad_ref[...] += dot(out_in, grad_mix, FIRST)
    grad_in = gin_ref[...]
    gain_ref[0:1, :] += jnp.sum(grad_in * scaled, 0, keepdims=True)
    grad_gated = inv_gate * (
        grad_in * chan_ref[1:2] - scaled * inv_gate * (cross * (1.0 / inner_all))
    )
    gy_ref[...] = grad_gated * active
    grad_z = (grad_gated * y_flat * (sig * (1.0 + gate_in * (1.0 - sig)))).astype(jnp.bfloat16)
    gz_ref[...] = grad_z
    wz_grad_ref[...] += dot(normed_ref[...], grad_z, FIRST)


def bwd_kernel(
    place_ref, cols_ref, seg_ref, normed_ref, conv_in_ref, dt_ref, pre_ref, y_ref, gy_ref, gz_ref,
    carried_ref, wcat_ref, conv_ref, head_ref, spread_ref, chan_ref, *refs,
    heads, inner, conv_width,
):
    (ext_ref, flow_ref), refs = refs[-2:], refs[:-2]
    sums_of, outs = split_refs(refs, 5)
    sent_ref, kept_ref, wx_grad_ref, wbc_grad_ref, wdt_grad_ref, conv_grad_ref, head_grad_ref = outs
    begin_sums((wx_grad_ref, wbc_grad_ref, wdt_grad_ref, conv_grad_ref, head_grad_ref), sums_of)

    @pl.when(pl.program_id(0) == 0)
    def _():
        ext_ref[SPAN : SPAN + 8, :] = jnp.zeros((8, conv_width), jnp.float32)
        flow_ref[...] = jnp.zeros_like(flow_ref)

    cols = cols_ref[...]
    pre = pre_ref[...]
    sig = sigmoid(pre)
    active = pre * sig
    slope = sig * (1.0 + pre * (1.0 - sig))
    x_conv = active[:, :inner]
    states = (conv_width - inner) // 2
    b_low = active[:, inner : inner + states].astype(jnp.bfloat16)
    c_low = active[:, inner + states :].astype(jnp.bfloat16)
    lower = lower_ones()
    spread = spread_ref[...]
    head_rows = head_ref[...]
    dt_in, step, falls, falls_t, step_x, in_x, out_x, linked = span_decays(
        dt_ref[...], cols, seg_ref[0], head_rows, spread, lower
    )
    kernel = dot(c_low, b_low, LAST)
    inputs = (step_x * x_conv).astype(jnp.bfloat16)
    grad_y = gy_ref[...]
    grad_scan = grad_y.astype(jnp.bfloat16)
    size = inner // heads
    group = LANES // size
    lane_head = lax.broadcasted_iota(jnp.int32, (SPAN, LANES), 1) // size
    grad_kernel = None
    grad_inputs = []
    for first in range(0, heads, group):
        at = first * size
        total = None
        for head in range(first, first + group):
            decay = jnp.exp(
                jnp.where(linked, falls[:, head : head + 1] - falls_t[head : head + 1, :], FAR)
            )
            mixing = (kernel * decay).astype(jnp.bfloat16)
            here = lane_head == head - first
            own = jnp.where(here, grad_scan[:, at : at + LANES], 0).astype(jnp.bfloat16)
            grad_part = dot(own, inputs[:, at : at + LANES], LAST) * decay
            grad_kernel = grad_part if grad_kernel is None else grad_kernel + grad_part
            part = dot(mixing, own, FIRST)
            total = part if total is None else total + part
        grad_inputs.append(total)
    flow = flow_ref[...]
    flow_low = flow.astype(jnp.bfloat16)
    grad_inputs = jnp.concatenate(grad_inputs, 1) + in_x * dot(b_low, flow_low)
    grad_kernel = grad_kernel.astype(jnp.bfloat16)
    inputs_wide = inputs.astype(jnp.float32)
    leaving, leaving_rest = parts_of(out_x * grad_scan.astype(jnp.float32), 2)
    entering = (in_x * inputs_wide).astype(jnp.bfloat16)
    grad_c = dot(grad_kernel, b_low) + dot(leaving, carried_ref[0], LAST)
    grad_b = dot(grad_kernel, c_low, FIRST) + dot(entering, flow_low, LAST)
    grad_carried = dot(c_low, leaving, FIRST) + dot(c_low, leaving_rest, FIRST)
    flow = out_x[SPAN - 1 : SPAN] * flow + grad_carried
    flow_ref[...] = flow
    crossing = jnp.sum(flow * carried_ref[0].astype(jnp.float32), 0, keepdims=True)
    crossing = dot_right_exact(jnp.broadcast_to(crossing, (8, inner)), spread, LAST)
    scanned = y_ref[...] - chan_ref[0:1] * x_conv
    grad_log = dot_right_exact(
        grad_scan.astype(jnp.float32) * scanned - inputs_wide * grad_inputs, spread, LAST
    )
    earlier = as_low(jnp.logical_not(upper_ones()))
    rate_sum = crossing[0:1] - dot_left_exact(earlier, grad_log, 3)
    grad_step = dot_right_exact(grad_inputs * x_conv, spread, LAST) + rate_sum * head_rows[1:2]
    grad_dt = grad_step * sigmoid(dt_in)
    head_grad_ref[0:1, :] += jnp.sum(grad_dt, 0, keepdims=True)
    head_grad_ref[1:2, :] += jnp.sum(rate_sum * step, 0, keepdims=True) * head_rows[1:2]
    grad_x = grad_y * chan_ref[0:1] + grad_inputs * step_x
    conv_grad_ref[5:6, 0:inner] += jnp.sum(grad_y * x_conv, 0, keepdims=True)
    grad_pre = jnp.concatenate([grad_x, grad_b, grad_c], 1) * slope
    conv_in = conv_in_ref[...]
    ext_ref[0:SPAN, :] = grad_pre
    grad_conv_in = conv_ref[0:1] * grad_pre
    conv_grad_ref[0:1, :] += jnp.sum(grad_pre * conv_in, 0, keepdims=True)
    conv_grad_ref[4:5, :] += jnp.sum(grad_pre, 0, keepdims=True)
    for lag in range(1, 4):
        term = ext_ref[lag : lag + SPAN, :] * cols[:, 7 + lag : 8 + lag]
        grad_conv_in = grad_conv_in + conv_ref[lag : lag + 1] * term
        conv_grad_ref[lag : lag + 1, :] += jnp.sum(term * conv_in, 0, keepdims=True)
    ext_ref[SPAN : SPAN + 8, :] = grad_pre[0:8]
    conv_low = grad_conv_in.astype(jnp.bfloat16)
    dt_low = grad_dt.astype(jnp.bfloat16)
    low = jnp.concatenate([conv_low, gz_ref[...], dt_low], 1)
    store_halves(place_ref, dot(low, wcat_ref[...], LAST), sent_ref, kept_ref)
    normed = normed_ref[...]
    wx_grad_ref[...] += dot(normed, conv_low[:, :inner], FIRST)
    wbc_grad_ref[...] += dot(normed, conv_low[:, inner:], FIRST)
    wdt_grad_ref[...] += dot(dt_low, normed, FIRST)


def upper_ones():
    down = lax.broadcasted_iota(jnp.int32, (SPAN, SPAN), 0)
    across = lax.broadcasted_iota(jnp.int32, (SPAN, SPAN), 1)
    return down <= across


def output_kernel(place_ref, own_ref, other_ref, hid_ref, cols_ref, *refs):
    out_ref = refs[-1]

    def write(values):
        out_ref[...] = (hid_ref[...].astype(jnp.float32) + cols_ref[:, 4:5] * values).astype(
            jnp.bfloat16
        )

    join_columns(place_ref, own_ref, other_ref, write)


def finish_kernel(place_ref, own_ref, other_ref, hid_ref, cot_ref, gain_ref, *refs):
    out_ref = refs[-1]
    hid = hid_ref[...].astype(jnp.float32)
    inv_rms = lax.rsqrt(jnp.mean(hid * hid, -1, keepdims=True) + EPS)

    def write(values):
        weighted = values * gain_ref[...]
        inner = jnp.mean(weighted * hid, -1, keepdims=True)
        out_ref[...] = (
            cot_ref[...].astype(jnp.float32)
            + inv_rms * weighted
            - hid * (inv_rms * inv_rms * inv_rms * inner)
        )

    join_columns(place_ref, own_ref, other_ref, write)


def partners(count, step):
    return [(place, place ^ step) for place in range(count)]


def steps_of(count):
    return [1 << level for level in range((count - 1).bit_length())]


def take_half(values, which):
    half = values.shape[0] // 2
    return lax.dynamic_slice_in_dim(values, which * half, half, 0)


def join_halves(own, other, mine):
    return jnp.where(
        mine == 0, jnp.concatenate([own, other], 0), jnp.concatenate([other, own], 0)
    )


def axis_scatter(values, axis, count, order):
    place = lax.axis_index(axis)
    for step in order:
        mine = (place // step) % 2
        sent = lax.ppermute(take_half(values, 1 - mine), axis, partners(count, step))
        values = take_half(values, mine) + sent
    return values


def axis_gather(values, axis, count, order):
    place = lax.axis_index(axis)
    for step in reversed(order):
        other = lax.ppermute(values, axis, partners(count, step))
        values = join_halves(values, other, (place // step) % 2)
    return values


def dp_order(count, first):
    order = steps_of(count)
    return order[first:2] + order[:first] + order[2:]


def together(*values):
    return lax.optimization_barrier(values)


def chip_sum(sent, kept, count):
    return kept + lax.ppermute(sent, "tensor", partners(count, 1))


def far_sum(values, count):
    for step in steps_of(count)[1:]:
        values = values + lax.ppermute(values, "tensor", partners(count, step))
    return values


def chip_other(values, count):
    return lax.ppermute(values, "tensor", partners(count, 1))


def pad_rows(values, multiple):
    return jnp.pad(values, ((0, -values.shape[0] % multiple), (0, 0)))


def call(kernel, grid, prefetch, ins, in_specs, outs, out_specs, scratch, flops, alias=None):
    moved = sum(a.size * a.dtype.itemsize for a in ins) + sum(
        o.size * o.dtype.itemsize for o in outs
    )
    return pl.pallas_call(
        kernel,
        grid_spec=pltpu.PrefetchScalarGridSpec(
            num_scalar_prefetch=len(prefetch),
            grid=grid,
            in_specs=in_specs,
            out_specs=out_specs,
            scratch_shapes=scratch,
        ),
        out_shape=outs,
        input_output_aliases=alias or {},
        cost_estimate=pl.CostEstimate(flops=flops, bytes_accessed=moved, transcendentals=0),
    )(*prefetch, *ins)


def per_device(
    n_dp,
    n_tensor,
    hidden,
    cotangent,
    seg_ids,
    counts,
    norm_gain,
    w_x,
    w_z,
    w_dt,
    w_bc,
    conv_x,
    conv_x_bias,
    conv_bc,
    conv_bc_bias,
    dt_bias,
    a_log,
    d_skip,
    gate_gain,
    w_out,
):
    f32, bf16 = jnp.float32, jnp.bfloat16
    rows, width = hidden.shape
    bc_width = w_bc.shape[1]
    states = bc_width // 2
    heads = w_dt.shape[1]
    inner = w_x.shape[1]
    taps = conv_x.shape[0]
    size = inner // heads
    spans = rows // SPAN
    half_spans = spans // 2
    conv_width = inner + bc_width
    all_width = conv_width + inner + LANES
    mine = lax.axis_index("tensor") % 2
    positions = jnp.arange(rows)
    seg_spans = seg_ids.reshape(spans, SPAN)
    seg_end = seg_spans[:, -1:]
    seg_prev = jnp.concatenate([jnp.full((1, 1), -1, jnp.int32), seg_end[:-1]], 0)

    def conv_link(lag):
        ahead = jnp.concatenate([jnp.full((lag,), -1, jnp.int32), seg_ids[:-lag]])
        return ahead == seg_ids

    def conv_link_next(lag):
        behind = jnp.concatenate([seg_ids[lag:], jnp.full((lag,), -1, jnp.int32)])
        return behind == seg_ids

    cols = jnp.stack(
        [
            seg_ids.astype(f32),
            conv_link(1).astype(f32),
            conv_link(2).astype(f32),
            conv_link(3).astype(f32),
            (positions < counts[0]).astype(f32),
            (seg_spans == seg_end).reshape(rows).astype(f32),
            (seg_spans == seg_prev).reshape(rows).astype(f32),
            jnp.zeros((rows,), f32),
            conv_link_next(1).astype(f32),
            conv_link_next(2).astype(f32),
            conv_link_next(3).astype(f32),
        ],
        1,
    )
    cols = jnp.pad(cols, ((0, 0), (0, 16 - cols.shape[1])))
    seg_rows = seg_spans.astype(f32)[:, None, :]
    w_cat = jnp.concatenate([w_x, w_bc, w_z, jnp.pad(w_dt, ((0, 0), (0, LANES - heads)))], 1)
    conv_rows = jnp.concatenate(
        [
            jnp.concatenate([conv_x, conv_bc], 1),
            jnp.concatenate([conv_x_bias, conv_bc_bias])[None],
        ],
        0,
    )
    conv_rows = jnp.pad(conv_rows, ((0, 8 - conv_rows.shape[0]), (0, 0)))
    head_rows = jnp.pad(
        jnp.stack([dt_bias, -jnp.exp(a_log)], 0), ((0, 6), (0, LANES - heads))
    )
    spread = (jnp.arange(LANES)[:, None] == jnp.arange(inner)[None, :] // size).astype(bf16)
    chan = jnp.pad(jnp.stack([jnp.repeat(d_skip, size), gate_gain], 0), ((0, 6), (0, 0)))
    gain = norm_gain[None]

    def shape(*dims, dtype=f32):
        return jax.ShapeDtypeStruct(dims, dtype)

    def whole(array):
        return pl.BlockSpec(array.shape, lambda *_: (0,) * len(array.shape))

    def fixed(*dims):
        return pl.BlockSpec(dims, lambda *_: (0,) * len(dims))

    def local(columns):
        return pl.BlockSpec((SPAN, columns), lambda i, *_: (i, 0))

    def back(columns):
        return pl.BlockSpec((SPAN, columns), lambda i, *_: (half_spans - 1 - i, 0))

    place = mine.astype(jnp.int32).reshape(1)
    half_rows = rows // 2
    grid = (half_spans,)

    def forward(half):
        base = half * half_spans
        full = lambda columns: pl.BlockSpec((SPAN, columns), lambda i: (base + i, 0))
        return call(
            functools.partial(fwd_kernel, heads=heads, inner=inner, conv_width=conv_width),
            grid,
            (),
            (
                hidden, cotangent, cols, seg_rows, gain, w_cat, w_out, conv_rows, head_rows,
                spread, chan,
            ),
            [
                full(width), full(width), full(16),
                pl.BlockSpec((1, 1, SPAN), lambda i: (base + i, 0, 0)),
            ]
            + [whole(a) for a in (gain, w_cat, w_out, conv_rows, head_rows, spread, chan)],
            (
                shape(half_rows, width, dtype=bf16),
                shape(half_rows, conv_width),
                shape(half_rows, inner),
                shape(half_rows, LANES),
                shape(half_rows, conv_width),
                shape(half_rows, inner),
                shape(half_rows, inner),
                shape(half_spans, states, inner, dtype=bf16),
                shape(half_spans, 2, SPAN),
            ),
            [
                local(width), local(conv_width), local(inner), local(LANES), local(conv_width),
                local(inner), local(inner),
                pl.BlockSpec((1, states, inner), lambda i: (i, 0, 0)),
                pl.BlockSpec((1, 2, SPAN), lambda i: (i, 0, 0)),
            ],
            [pltpu.VMEM((SPAN + 8, conv_width), f32), pltpu.VMEM((states, inner), f32)],
            12_000_000_000,
        )

    def tensor_small(sums):
        for step in steps_of(n_tensor):
            sums = sums + lax.ppermute(sums, "tensor", partners(n_tensor, step))
        return sums

    def gate(half, sums, gate_in, y_flat, grad_in, normed, before):
        base = half * half_spans
        full = lambda columns: pl.BlockSpec((SPAN, columns), lambda i, s: (base + i, 0))
        totals = (shape(inner, width), shape(width, inner), shape(8, inner))
        return call(
            functools.partial(gate_kernel, inner=inner, inner_all=inner * n_tensor),
            grid,
            (place,),
            (sums, gate_in, y_flat, grad_in, cotangent, cols, normed, w_out, chan) + before,
            [
                pl.BlockSpec((1, 2, SPAN), lambda i, s: (i, 0, 0)),
                local(inner), local(inner), local(inner), full(width), full(16),
                local(width), whole(w_out), whole(chan),
            ]
            + [whole(a) for a in before],
            (
                shape(half_rows, width // 2),
                shape(half_rows, width // 2),
                shape(half_rows, inner),
                shape(half_rows, inner, dtype=bf16),
            )
            + totals,
            [local(width // 2), local(width // 2), local(inner), local(inner)]
            + [fixed(*a.shape) for a in totals],
            [],
            8_000_000_000,
        )

    def backward(half, normed, conv_in, dt_part, pre, y_flat, grad_y, grad_z, carried, before):
        base = half * half_spans
        turn = lambda i: base + half_spans - 1 - i
        full = lambda columns: pl.BlockSpec((SPAN, columns), lambda i, s: (turn(i), 0))
        totals = (
            shape(width, inner),
            shape(width, bc_width),
            shape(LANES, width),
            shape(8, conv_width),
            shape(8, LANES),
        )
        return call(
            functools.partial(bwd_kernel, heads=heads, inner=inner, conv_width=conv_width),
            grid,
            (place,),
            (
                cols, seg_rows, normed, conv_in, dt_part, pre, y_flat, grad_y, grad_z, carried,
                w_cat, conv_rows, head_rows, spread, chan,
            )
            + before,
            [
                full(16), pl.BlockSpec((1, 1, SPAN), lambda i, s: (turn(i), 0, 0)),
                back(width), back(conv_width), back(LANES), back(conv_width), back(inner),
                back(inner), back(inner),
                pl.BlockSpec((1, states, inner), lambda i, s: (half_spans - 1 - i, 0, 0)),
            ]
            + [whole(a) for a in (w_cat, conv_rows, head_rows, spread, chan)]
            + [whole(a) for a in before],
            (shape(half_rows, width // 2), shape(half_rows, width // 2)) + totals,
            [back(width // 2), back(width // 2)] + [fixed(*a.shape) for a in totals],
            [pltpu.VMEM((SPAN + 8, conv_width), f32), pltpu.VMEM((states, inner), f32)],
            20_000_000_000,
        )

    def placed(kernel, half, own, other, extras, extra_specs, dtype, before):
        base = half * half_spans
        full = lambda columns: pl.BlockSpec((SPAN, columns), lambda i, s: (base + i, 0))
        specs = [whole(a) if spec is None else full(spec) for a, spec in zip(extras, extra_specs)]
        (made,) = call(
            kernel,
            grid,
            (place,),
            (own, other) + extras + before,
            [local(width // 2)] * 2 + specs + [pl.BlockSpec(memory_space=pl.ANY)] * len(before),
            (shape(rows, width, dtype=dtype),),
            [full(width)],
            [],
            3_000_000_000,
            {3 + len(extras): 0} if before else None,
        )
        return made

    normed_a, conv_a, z_a, dt_a, pre_a, y_a, gin_a, carried_a, sums_a = forward(0)
    normed_b, conv_b, z_b, dt_b, pre_b, y_b, gin_b, carried_b, sums_b = forward(1)
    sums_a = tensor_small(sums_a)
    sums_b = tensor_small(sums_b)
    sent, kept, gy_a, gz_a, *gate_sums = gate(0, sums_a, z_a, y_a, gin_a, normed_a, ())
    mixed_a = chip_sum(sent, kept, n_tensor)
    mixed_a, sums_b = together(mixed_a, sums_b)
    far_mixed_a = far_sum(mixed_a, n_tensor)
    sent, kept, gy_b, gz_b, *gate_sums = gate(
        1, sums_b, z_b, y_b, gin_b, normed_b, tuple(gate_sums)
    )
    part_out, part_z, gate_grad = gate_sums
    mixed_b = chip_sum(sent, kept, n_tensor)
    mixed_b, gy_a = together(mixed_b, gy_a)
    far_mixed_b = far_sum(mixed_b, n_tensor)
    sent_a, kept_a, *bwd_sums = backward(
        0, normed_a, conv_a, dt_a, pre_a, y_a, gy_a, gz_a, carried_a, ()
    )
    normed_sum_a = chip_sum(sent_a, kept_a, n_tensor)
    order_y, order_z = dp_order(n_dp, 0), dp_order(n_dp, 1)
    out_parts = axis_scatter(part_out, "dp", n_dp, order_y[:1])
    z_parts = axis_scatter(part_z, "dp", n_dp, order_z[:1])
    normed_sum_a, far_mixed_a, out_parts, z_parts, gy_b = together(
        normed_sum_a, far_mixed_a, out_parts, z_parts, gy_b
    )
    far_normed_a = far_sum(normed_sum_a, n_tensor)
    out_parts = axis_scatter(out_parts, "dp", n_dp, order_y[1:2])
    z_parts = axis_scatter(z_parts, "dp", n_dp, order_z[1:2])
    sent_b, kept_b, wx_part, wbc_part, wdt_part, conv_grad, head_grad = backward(
        1, normed_b, conv_b, dt_b, pre_b, y_b, gy_b, gz_b, carried_b, tuple(bwd_sums)
    )
    sent_b, far_mixed_b, out_parts, z_parts, wx_part, wbc_part = together(
        sent_b, far_mixed_b, out_parts, z_parts, wx_part, wbc_part
    )
    far_normed_b = far_sum(chip_sum(sent_b, kept_b, n_tensor), n_tensor)
    wide = lambda values: values.astype(f32)
    norm_grad = (
        jnp.sum(wx_part * wide(w_x), 1)
        + jnp.sum(part_z * wide(w_z), 1)
        + jnp.sum(wbc_part * wide(w_bc), 1)
        + jnp.sum(wdt_part[:heads].T * wide(w_dt), 1)
    ) / norm_gain

    def widen(values, columns):
        flat = values.reshape(-1)
        return jnp.pad(flat, (0, -flat.size % columns)).reshape(-1, columns)

    bc_small = jnp.concatenate([conv_grad[:5, inner:].reshape(-1), norm_grad])
    bc_parts = pad_rows(jnp.concatenate([wbc_part, widen(bc_small, bc_width)], 0), 16 * n_dp)
    x_small = jnp.concatenate(
        [
            conv_grad[:5, :inner].reshape(-1),
            gate_grad[0],
            head_grad[0, :heads],
            head_grad[1, :heads],
            jnp.sum(conv_grad[5, :inner].reshape(heads, size), 1),
            wdt_part[:heads].reshape(-1),
        ]
    )
    x_parts = pad_rows(jnp.concatenate([wx_part, widen(x_small, inner)], 0), 8 * n_dp)
    x_parts = axis_scatter(x_parts, "dp", n_dp, order_y)
    bc_parts = axis_scatter(bc_parts, "tensor", n_tensor, [1])
    bc_parts = axis_scatter(bc_parts, "dp", n_dp, order_z)
    out_parts = axis_scatter(out_parts, "dp", n_dp, order_y[2:])
    z_parts = axis_scatter(z_parts, "dp", n_dp, order_z[2:])
    for step in steps_of(n_tensor)[1:]:
        bc_parts = bc_parts + lax.ppermute(bc_parts, "tensor", partners(n_tensor, step))
    out_grad = axis_gather(out_parts, "dp", n_dp, order_y)
    z_grad = axis_gather(z_parts, "dp", n_dp, order_z)
    x_parts = axis_gather(x_parts, "dp", n_dp, order_y)
    bc_parts = axis_gather(bc_parts, "dp", n_dp, order_z)
    bc_parts = axis_gather(bc_parts, "tensor", n_tensor, [1])
    output = placed(
        output_kernel, 0, far_mixed_a, chip_other(far_mixed_a, n_tensor), (hidden, cols),
        (width, 16), bf16, (),
    )
    output = placed(
        output_kernel, 1, far_mixed_b, chip_other(far_mixed_b, n_tensor), (hidden, cols),
        (width, 16), bf16, (output,),
    )
    grad_hidden = placed(
        finish_kernel, 0, far_normed_a, chip_other(far_normed_a, n_tensor),
        (hidden, cotangent, gain), (width, width, None), f32, (),
    )
    grad_hidden = placed(
        finish_kernel, 1, far_normed_b, chip_other(far_normed_b, n_tensor),
        (hidden, cotangent, gain), (width, width, None), f32, (grad_hidden,),
    )
    x_small = x_parts[width:].reshape(-1)
    bc_small = bc_parts[width:].reshape(-1)
    at = (taps + 1) * inner
    heads_at = at + inner
    dt_at = heads_at + 3 * heads
    bc_at = (taps + 1) * bc_width
    return (
        output,
        grad_hidden,
        bc_small[bc_at : bc_at + width],
        x_parts[:width],
        z_grad,
        x_small[dt_at : dt_at + heads * width].reshape(heads, width).T,
        bc_parts[:width],
        x_small[: taps * inner].reshape(taps, inner),
        x_small[taps * inner : at],
        bc_small[: taps * bc_width].reshape(taps, bc_width),
        bc_small[taps * bc_width : bc_at],
        x_small[heads_at : heads_at + heads],
        x_small[heads_at + heads : heads_at + 2 * heads],
        x_small[heads_at + 2 * heads : dt_at],
        x_small[at : at + inner],
        out_grad,
    )


def solution(mesh):
    return jax.shard_map(
        functools.partial(per_device, mesh.shape["dp"], mesh.shape["tensor"]),
        mesh=mesh,
        in_specs=(
            P("dp", None),
            P("dp", None),
            P("dp"),
            P("dp"),
            P(),
            P(None, "tensor"),
            P(None, "tensor"),
            P(None, "tensor"),
            P(),
            P(None, "tensor"),
            P("tensor"),
            P(),
            P(),
            P("tensor"),
            P("tensor"),
            P("tensor"),
            P("tensor"),
            P("tensor", None),
        ),
        out_specs=(
            P("dp", None),
            P("dp", None),
            P(),
            P(None, "tensor"),
            P(None, "tensor"),
            P(None, "tensor"),
            P(),
            P(None, "tensor"),
            P("tensor"),
            P(),
            P(),
            P("tensor"),
            P("tensor"),
            P("tensor"),
            P("tensor"),
            P("tensor", None),
        ),
        check_vma=False,
    )
```

```python
import functools

import jax
import jax.numpy as jnp
from jax import lax
from jax.experimental import pallas as pl
from jax.experimental.pallas import tpu as pltpu
from jax.sharding import PartitionSpec as P

SPAN = 256
LANES = 128
EPS = 1e-05
FAR = -10000.0
FIRST = ((0,), (0,))
LAST = ((1,), (1,))


def dot(left, right, dims=((1,), (0,))):
    return lax.dot_general(left, right, (dims, ((), ())), preferred_element_type=jnp.float32)


def parts_of(values, count):
    parts = []
    for _ in range(count):
        part = values.astype(jnp.bfloat16)
        values = values - part.astype(jnp.float32)
        parts.append(part)
    return parts


def dot_left_exact(left, values, count):
    total = None
    for part in parts_of(values, count):
        product = dot(left, part)
        total = product if total is None else total + product
    return total


def dot_right_exact(values, right, dims):
    total = None
    for part in parts_of(values, 2):
        product = dot(part, right, dims)
        total = product if total is None else total + product
    return total


def sigmoid(values):
    return 1.0 / (1.0 + jnp.exp(-values))


def softplus(values):
    return jnp.maximum(values, 0.0) + jnp.log1p(jnp.exp(-jnp.abs(values)))


def lower_ones():
    down = lax.broadcasted_iota(jnp.int32, (SPAN, SPAN), 0)
    across = lax.broadcasted_iota(jnp.int32, (SPAN, SPAN), 1)
    return down >= across


def flag_columns(rows):
    blank = jnp.zeros((LANES - rows.shape[0], rows.shape[1]), jnp.float32)
    return jnp.concatenate([rows, blank], 0).T


def as_low(flags):
    return jnp.where(flags, 1.0, 0.0).astype(jnp.bfloat16)


def span_decays(dt_part, cols, seg_row, head_rows, spread, lower):
    dt_in = dt_part + head_rows[0:1]
    step = softplus(dt_in)
    falls = dot_left_exact(as_low(lower), step * head_rows[1:2], 3)
    falls_t = falls.T
    decay_in = jnp.exp(falls[SPAN - 1 : SPAN] - falls) * cols[:, 5:6]
    decay_out = jnp.exp(falls) * cols[:, 6:7]
    linked = lower & (cols[:, 0:1] == seg_row)
    wide = lambda values: dot_right_exact(values, spread, ((1,), (0,)))
    return dt_in, step, falls, falls_t, wide(step), wide(decay_in), wide(decay_out), linked


def fwd_kernel(
    hid_ref, cot_ref, flags_ref, gain_ref, wcat_ref, wout_ref, conv_ref, head_ref,
    spread_ref, chan_ref, normed_ref, conv_in_ref, z_ref, dt_ref, pre_ref, y_ref, gin_ref,
    carried_ref, sums_ref, ext_ref, state_ref, *, heads, inner, conv_width,
):
    @pl.when(pl.program_id(0) == 0)
    def _():
        ext_ref[0:8, :] = jnp.zeros((8, conv_width), jnp.float32)
        state_ref[...] = jnp.zeros_like(state_ref)

    cols = flag_columns(flags_ref[...])
    hid = hid_ref[...].astype(jnp.float32)
    inv_rms = lax.rsqrt(jnp.mean(hid * hid, -1, keepdims=True) + EPS)
    normed = (hid * inv_rms * gain_ref[...]).astype(jnp.bfloat16)
    normed_ref[...] = normed
    conv_in = dot(normed, wcat_ref[:, 0:conv_width])
    gate_in = dot(normed, wcat_ref[:, conv_width : conv_width + inner])
    dt_part = dot(normed, wcat_ref[:, conv_width + inner :])
    conv_in_ref[...] = conv_in
    z_ref[...] = gate_in
    dt_ref[...] = dt_part
    ext_ref[8 : 8 + SPAN, :] = conv_in
    pre = conv_ref[4:5] + conv_ref[0:1] * conv_in
    for lag in range(1, 4):
        earlier = ext_ref[8 - lag : 8 - lag + SPAN, :]
        pre = pre + conv_ref[lag : lag + 1] * (earlier * cols[:, lag : lag + 1])
    ext_ref[0:8, :] = conv_in[SPAN - 8 :]
    pre_ref[...] = pre
    active = pre * sigmoid(pre)
    x_conv = active[:, :inner]
    states = (conv_width - inner) // 2
    b_low = active[:, inner : inner + states].astype(jnp.bfloat16)
    c_low = active[:, inner + states :].astype(jnp.bfloat16)
    lower = lower_ones()
    _, _, falls, falls_t, step_x, in_x, out_x, linked = span_decays(
        dt_part, cols, flags_ref[0:1], head_ref[...], spread_ref[...], lower
    )
    kernel = dot(c_low, b_low, LAST)
    inputs = (step_x * x_conv).astype(jnp.bfloat16)
    size = inner // heads
    group = LANES // size
    lane_head = lax.broadcasted_iota(jnp.int32, (SPAN, LANES), 1) // size
    local = []
    for first in range(0, heads, group):
        at = first * size
        total = None
        for head in range(first, first + group):
            decay = jnp.exp(
                jnp.where(linked, falls[:, head : head + 1] - falls_t[head : head + 1, :], FAR)
            )
            mixing = (kernel * decay).astype(jnp.bfloat16)
            own = jnp.where(lane_head == head - first, inputs[:, at : at + LANES], 0)
            part = dot(mixing, own.astype(jnp.bfloat16))
            total = part if total is None else total + part
        local.append(total)
    local = jnp.concatenate(local, 1)
    carried = state_ref[...].astype(jnp.bfloat16)
    carried_ref[0] = carried
    y_flat = local + out_x * dot(c_low, carried) + chan_ref[0:1] * x_conv
    entering = (inputs.astype(jnp.float32) * in_x).astype(jnp.bfloat16)
    state_ref[...] = out_x[SPAN - 1 : SPAN] * state_ref[...] + dot(b_low, entering, FIRST)
    y_ref[...] = y_flat
    gated = y_flat * (gate_in * sigmoid(gate_in))
    grad_mix = (cols[:, 4:5] * cot_ref[...].astype(jnp.float32)).astype(jnp.bfloat16)
    grad_in = dot(grad_mix, wout_ref[...], LAST)
    gin_ref[...] = grad_in
    squares = jnp.sum(gated * gated, -1, keepdims=True)
    cross = jnp.sum(grad_in * chan_ref[1:2] * gated, -1, keepdims=True)
    lane = lax.broadcasted_iota(jnp.int32, (SPAN, LANES), 1)
    sums_ref[0] = jnp.where(lane == 0, squares, cross).T[0:2]


def split_refs(refs, count, outs):
    return (refs[:count], refs[count:]) if len(refs) > outs else ((), refs)


def begin_sums(targets, sources):
    @pl.when(pl.program_id(0) == 0)
    def _():
        for place, target in enumerate(targets):
            target[...] = sources[place][...] if sources else jnp.zeros_like(target)


def store_halves(place_ref, values, sent_ref, kept_ref):
    half = values.shape[1] // 2

    @pl.when(place_ref[0] == 0)
    def _():
        kept_ref[...] = values[:, :half]
        sent_ref[...] = values[:, half:]

    @pl.when(place_ref[0] == 1)
    def _():
        kept_ref[...] = values[:, half:]
        sent_ref[...] = values[:, :half]


def join_columns(place_ref, own_ref, other_ref, write):
    own, other = own_ref[...], other_ref[...]

    @pl.when(place_ref[0] == 0)
    def _():
        write(jnp.concatenate([own, other], 1))

    @pl.when(place_ref[0] == 1)
    def _():
        write(jnp.concatenate([other, own], 1))


def gate_kernel(
    place_ref, sums_ref, z_ref, y_ref, gin_ref, cot_ref, flags_ref, normed_ref, wout_ref, chan_ref,
    *refs, inner, inner_all,
):
    sums_of, outs = split_refs(refs, 2, 6)
    sent_ref, kept_ref, gy_ref, gz_ref, early_ref, gain_ref = outs
    begin_sums((early_ref, gain_ref), sums_of)
    live = flag_columns(flags_ref[...])[:, 4:5]

    sums = sums_ref[0]
    copies = inner // LANES
    over = lambda row: jnp.concatenate([jnp.broadcast_to(row, (LANES, SPAN)).T] * copies, 1)
    squares, cross = over(sums[0:1]), over(sums[1:2])
    inv_gate = lax.rsqrt(squares / inner_all + EPS)
    gate_in = z_ref[...]
    y_flat = y_ref[...]
    sig = sigmoid(gate_in)
    active = gate_in * sig
    gated = y_flat * active
    scaled = gated * inv_gate
    out_in = (scaled * chan_ref[1:2]).astype(jnp.bfloat16)
    store_halves(place_ref, dot(out_in, wout_ref[...]), sent_ref, kept_ref)
    grad_mix = (live * cot_ref[...].astype(jnp.float32)).astype(jnp.bfloat16)
    early_ref[0:inner, :] += dot(out_in, grad_mix, FIRST)
    grad_in = gin_ref[...]
    gain_ref[0:1, :] += jnp.sum(grad_in * scaled, 0, keepdims=True)
    grad_gated = inv_gate * (
        grad_in * chan_ref[1:2] - scaled * inv_gate * (cross * (1.0 / inner_all))
    )
    gy_ref[...] = grad_gated * active
    grad_z = (grad_gated * y_flat * (sig * (1.0 + gate_in * (1.0 - sig)))).astype(jnp.bfloat16)
    gz_ref[...] = grad_z
    early_ref[inner : 2 * inner, :] += dot(grad_z, normed_ref[...], FIRST)


def bwd_kernel(
    place_ref, flags_ref, normed_ref, conv_in_ref, dt_ref, pre_ref, y_ref, gy_ref, gz_ref,
    carried_ref, wcat_ref, conv_ref, head_ref, spread_ref, chan_ref, *refs,
    heads, inner, conv_width,
):
    (ext_ref, flow_ref), refs = refs[-2:], refs[:-2]
    befores, outs = split_refs(refs, 5, 4)
    sent_ref, kept_ref, upper_ref, below_ref = outs
    begin_sums((upper_ref, below_ref), befores[:2])
    width = normed_ref.shape[1]
    top = width // 2
    small = below_ref.at[top:, :]

    @pl.when(pl.program_id(0) == 0)
    def _():
        ext_ref[SPAN : SPAN + 8, :] = jnp.zeros((8, conv_width), jnp.float32)
        flow_ref[...] = jnp.zeros_like(flow_ref)

    cols = flag_columns(flags_ref[...])
    pre = pre_ref[...]
    sig = sigmoid(pre)
    active = pre * sig
    slope = sig * (1.0 + pre * (1.0 - sig))
    x_conv = active[:, :inner]
    states = (conv_width - inner) // 2
    b_low = active[:, inner : inner + states].astype(jnp.bfloat16)
    c_low = active[:, inner + states :].astype(jnp.bfloat16)
    lower = lower_ones()
    spread = spread_ref[...]
    head_rows = head_ref[...]
    dt_in, step, falls, falls_t, step_x, in_x, out_x, linked = span_decays(
        dt_ref[...], cols, flags_ref[0:1], head_rows, spread, lower
    )
    kernel = dot(c_low, b_low, LAST)
    inputs = (step_x * x_conv).astype(jnp.bfloat16)
    grad_y = gy_ref[...]
    grad_scan = grad_y.astype(jnp.bfloat16)
    size = inner // heads
    group = LANES // size
    lane_head = lax.broadcasted_iota(jnp.int32, (SPAN, LANES), 1) // size
    grad_kernel = None
    grad_inputs = []
    for first in range(0, heads, group):
        at = first * size
        total = None
        for head in range(first, first + group):
            decay = jnp.exp(
                jnp.where(linked, falls[:, head : head + 1] - falls_t[head : head + 1, :], FAR)
            )
            mixing = (kernel * decay).astype(jnp.bfloat16)
            here = lane_head == head - first
            own = jnp.where(here, grad_scan[:, at : at + LANES], 0).astype(jnp.bfloat16)
            grad_part = dot(own, inputs[:, at : at + LANES], LAST) * decay
            grad_kernel = grad_part if grad_kernel is None else grad_kernel + grad_part
            part = dot(mixing, own, FIRST)
            total = part if total is None else total + part
        grad_inputs.append(total)
    flow = flow_ref[...]
    flow_low = flow.astype(jnp.bfloat16)
    grad_inputs = jnp.concatenate(grad_inputs, 1) + in_x * dot(b_low, flow_low)
    grad_kernel = grad_kernel.astype(jnp.bfloat16)
    inputs_wide = inputs.astype(jnp.float32)
    leaving, leaving_rest = parts_of(out_x * grad_scan.astype(jnp.float32), 2)
    entering = (in_x * inputs_wide).astype(jnp.bfloat16)
    grad_c = dot(grad_kernel, b_low) + dot(leaving, carried_ref[0], LAST)
    grad_b = dot(grad_kernel, c_low, FIRST) + dot(entering, flow_low, LAST)
    grad_carried = dot(c_low, leaving, FIRST) + dot(c_low, leaving_rest, FIRST)
    flow = out_x[SPAN - 1 : SPAN] * flow + grad_carried
    flow_ref[...] = flow
    crossing = jnp.sum(flow * carried_ref[0].astype(jnp.float32), 0, keepdims=True)
    crossing = dot_right_exact(jnp.broadcast_to(crossing, (8, inner)), spread, LAST)
    scanned = y_ref[...] - chan_ref[0:1] * x_conv
    grad_log = dot_right_exact(
        grad_scan.astype(jnp.float32) * scanned - inputs_wide * grad_inputs, spread, LAST
    )
    earlier = as_low(jnp.logical_not(upper_ones()))
    rate_sum = crossing[0:1] - dot_left_exact(earlier, grad_log, 3)
    grad_step = dot_right_exact(grad_inputs * x_conv, spread, LAST) + rate_sum * head_rows[1:2]
    grad_dt = grad_step * sigmoid(dt_in)
    small[7:8, 0:LANES] += jnp.sum(grad_dt, 0, keepdims=True)
    small[8:9, 0:LANES] += jnp.sum(rate_sum * step, 0, keepdims=True) * head_rows[1:2]
    grad_x = grad_y * chan_ref[0:1] + grad_inputs * step_x
    small[5:6, 0:inner] += jnp.sum(grad_y * x_conv, 0, keepdims=True)
    grad_pre = jnp.concatenate([grad_x, grad_b, grad_c], 1) * slope
    conv_in = conv_in_ref[...]
    ext_ref[0:SPAN, :] = grad_pre
    grad_conv_in = conv_ref[0:1] * grad_pre
    small[0:1, :] += jnp.sum(grad_pre * conv_in, 0, keepdims=True)
    small[4:5, :] += jnp.sum(grad_pre, 0, keepdims=True)
    for lag in range(1, 4):
        term = ext_ref[lag : lag + SPAN, :] * cols[:, 7 + lag : 8 + lag]
        grad_conv_in = grad_conv_in + conv_ref[lag : lag + 1] * term
        small[lag : lag + 1, :] += jnp.sum(term * conv_in, 0, keepdims=True)
    ext_ref[SPAN : SPAN + 8, :] = grad_pre[0:8]
    conv_low = grad_conv_in.astype(jnp.bfloat16)
    dt_low = grad_dt.astype(jnp.bfloat16)
    low = jnp.concatenate([conv_low, gz_ref[...], dt_low], 1)
    store_halves(place_ref, dot(low, wcat_ref[...], LAST), sent_ref, kept_ref)
    normed = normed_ref[...]
    upper_ref[...] += dot(normed[:, :top], conv_low, FIRST)
    below_ref[0:top, :] += dot(normed[:, top:], conv_low, FIRST)
    dt_grad = dot(dt_low, normed, FIRST)
    small[16 : 16 + heads, 0:inner] += dt_grad[0:heads, :inner]
    small[24 : 24 + heads, 0 : width - inner] += dt_grad[0:heads, inner:]

    if befores:
        early_ref, gate_grad_ref, gain_ref = befores[2:]

        @pl.when(pl.program_id(0) == pl.num_programs(0) - 1)
        def _():
            small[6:7, 0:inner] = gate_grad_ref[0:1, :]
            weights = wcat_ref[:, 0:conv_width].astype(jnp.float32)
            first = jnp.sum(upper_ref[...] * weights[:top], 1, keepdims=True)
            second = jnp.sum(below_ref[0:top, :] * weights[top:], 1, keepdims=True)
            dt_all = jnp.concatenate(
                [small[16 : 16 + heads, 0:inner], small[24 : 24 + heads, 0 : width - inner]], 1
            )
            blank = jnp.zeros((LANES - heads, width), jnp.float32)
            dt_all = jnp.concatenate([dt_all, blank], 0).T
            rest = jnp.concatenate([early_ref[inner : 2 * inner, :].T, dt_all], 1)
            third = jnp.sum(
                rest * wcat_ref[:, conv_width:].astype(jnp.float32), 1, keepdims=True
            )
            total = jnp.concatenate([first, second], 0) + third
            row = jnp.broadcast_to(total, (width, LANES)).T[0:1] / gain_ref[...]
            part = conv_width - inner
            for place in range(width // part):
                small[9 + place : 10 + place, inner:] = row[:, place * part : (place + 1) * part]


def upper_ones():
    down = lax.broadcasted_iota(jnp.int32, (SPAN, SPAN), 0)
    across = lax.broadcasted_iota(jnp.int32, (SPAN, SPAN), 1)
    return down <= across


def output_kernel(place_ref, own_ref, other_ref, hid_ref, flags_ref, *refs):
    out_ref = refs[-1]
    live = flag_columns(flags_ref[...])[:, 4:5]

    def write(values):
        out_ref[...] = (hid_ref[...].astype(jnp.float32) + live * values).astype(
            jnp.bfloat16
        )

    join_columns(place_ref, own_ref, other_ref, write)


def finish_kernel(place_ref, own_ref, other_ref, hid_ref, cot_ref, gain_ref, *refs):
    out_ref = refs[-1]
    hid = hid_ref[...].astype(jnp.float32)
    inv_rms = lax.rsqrt(jnp.mean(hid * hid, -1, keepdims=True) + EPS)

    def write(values):
        weighted = values * gain_ref[...]
        inner = jnp.mean(weighted * hid, -1, keepdims=True)
        out_ref[...] = (
            cot_ref[...].astype(jnp.float32)
            + inv_rms * weighted
            - hid * (inv_rms * inv_rms * inv_rms * inner)
        )

    join_columns(place_ref, own_ref, other_ref, write)


def partners(count, step):
    return [(place, place ^ step) for place in range(count)]


def steps_of(count):
    return [1 << level for level in range((count - 1).bit_length())]


def take_half(values, which):
    half = values.shape[0] // 2
    return lax.dynamic_slice_in_dim(values, which * half, half, 0)


def join_halves(own, other, mine):
    return jnp.where(
        mine == 0, jnp.concatenate([own, other], 0), jnp.concatenate([other, own], 0)
    )


def axis_scatter(values, axis, count, order):
    place = lax.axis_index(axis)
    for step in order:
        mine = (place // step) % 2
        sent = lax.ppermute(take_half(values, 1 - mine), axis, partners(count, step))
        values = take_half(values, mine) + sent
    return values


def half_sent(values, axis, count, step):
    mine = (lax.axis_index(axis) // step) % 2
    return lax.ppermute(take_half(values, 1 - mine), axis, partners(count, step))


def half_kept(values, axis, step):
    return take_half(values, (lax.axis_index(axis) // step) % 2)


def axis_gather(values, axis, count, order):
    place = lax.axis_index(axis)
    for step in reversed(order):
        other = lax.ppermute(values, axis, partners(count, step))
        values = join_halves(values, other, (place // step) % 2)
    return values


def dp_order(count, first):
    order = steps_of(count)
    return order[first:2] + order[:first] + order[2:]


def together(*values):
    return lax.optimization_barrier(values)


def chip_sum(sent, kept, count):
    return kept + lax.ppermute(sent, "tensor", partners(count, 1))


def far_sum(values, count):
    for step in steps_of(count)[1:]:
        values = values + lax.ppermute(values, "tensor", partners(count, step))
    return values


def chip_other(values, count):
    return lax.ppermute(values, "tensor", partners(count, 1))


def pad_rows(values, multiple):
    return jnp.pad(values, ((0, -values.shape[0] % multiple), (0, 0)))


def call(kernel, grid, prefetch, ins, in_specs, outs, out_specs, scratch, flops, alias=None):
    moved = sum(a.size * a.dtype.itemsize for a in ins) + sum(
        o.size * o.dtype.itemsize for o in outs
    )
    return pl.pallas_call(
        kernel,
        grid_spec=pltpu.PrefetchScalarGridSpec(
            num_scalar_prefetch=len(prefetch),
            grid=grid,
            in_specs=in_specs,
            out_specs=out_specs,
            scratch_shapes=scratch,
        ),
        out_shape=outs,
        input_output_aliases=alias or {},
        cost_estimate=pl.CostEstimate(flops=flops, bytes_accessed=moved, transcendentals=0),
    )(*prefetch, *ins)


def per_device(
    n_dp,
    n_tensor,
    hidden,
    cotangent,
    seg_ids,
    counts,
    norm_gain,
    w_x,
    w_z,
    w_dt,
    w_bc,
    conv_x,
    conv_x_bias,
    conv_bc,
    conv_bc_bias,
    dt_bias,
    a_log,
    d_skip,
    gate_gain,
    w_out,
):
    f32, bf16 = jnp.float32, jnp.bfloat16
    rows, width = hidden.shape
    bc_width = w_bc.shape[1]
    states = bc_width // 2
    heads = w_dt.shape[1]
    inner = w_x.shape[1]
    taps = conv_x.shape[0]
    size = inner // heads
    spans = rows // SPAN
    half_spans = spans // 2
    conv_width = inner + bc_width
    all_width = conv_width + inner + LANES
    mine = lax.axis_index("tensor") % 2
    positions = jnp.arange(rows)
    seg_spans = seg_ids.reshape(spans, SPAN)
    seg_end = seg_spans[:, -1:]
    seg_prev = jnp.concatenate([jnp.full((1, 1), -1, jnp.int32), seg_end[:-1]], 0)

    def conv_link(lag):
        ahead = jnp.concatenate([jnp.full((lag,), -1, jnp.int32), seg_ids[:-lag]])
        return ahead == seg_ids

    def conv_link_next(lag):
        behind = jnp.concatenate([seg_ids[lag:], jnp.full((lag,), -1, jnp.int32)])
        return behind == seg_ids

    flags = jnp.stack(
        [
            seg_ids.astype(f32),
            conv_link(1).astype(f32),
            conv_link(2).astype(f32),
            conv_link(3).astype(f32),
            (positions < counts[0]).astype(f32),
            (seg_spans == seg_end).astype(f32).reshape(rows),
            (seg_spans == seg_prev).astype(f32).reshape(rows),
            jnp.zeros((rows,), f32),
            conv_link_next(1).astype(f32),
            conv_link_next(2).astype(f32),
            conv_link_next(3).astype(f32),
        ]
        + [jnp.zeros((rows,), f32)] * 5,
        0,
    )
    w_cat = jnp.concatenate([w_x, w_bc, w_z, jnp.pad(w_dt, ((0, 0), (0, LANES - heads)))], 1)
    conv_rows = jnp.concatenate(
        [
            jnp.concatenate([conv_x, conv_bc], 1),
            jnp.concatenate([conv_x_bias, conv_bc_bias])[None],
        ],
        0,
    )
    conv_rows = jnp.pad(conv_rows, ((0, 8 - conv_rows.shape[0]), (0, 0)))
    head_rows = jnp.pad(
        jnp.stack([dt_bias, -jnp.exp(a_log)], 0), ((0, 6), (0, LANES - heads))
    )
    spread = (jnp.arange(LANES)[:, None] == jnp.arange(inner)[None, :] // size).astype(bf16)
    chan = jnp.pad(jnp.stack([jnp.repeat(d_skip, size), gate_gain], 0), ((0, 6), (0, 0)))
    gain = norm_gain[None]

    def shape(*dims, dtype=f32):
        return jax.ShapeDtypeStruct(dims, dtype)

    def whole(array):
        return pl.BlockSpec(array.shape, lambda *_: (0,) * len(array.shape))

    def fixed(*dims):
        return pl.BlockSpec(dims, lambda *_: (0,) * len(dims))

    def local(columns):
        return pl.BlockSpec((SPAN, columns), lambda i, *_: (i, 0))

    def back(columns):
        return pl.BlockSpec((SPAN, columns), lambda i, *_: (half_spans - 1 - i, 0))

    place = mine.astype(jnp.int32).reshape(1)
    half_rows = rows // 2
    grid = (half_spans,)

    def forward():
        full = lambda columns: pl.BlockSpec((SPAN, columns), lambda i: (i, 0))
        return call(
            functools.partial(fwd_kernel, heads=heads, inner=inner, conv_width=conv_width),
            (spans,),
            (),
            (
                hidden, cotangent, flags, gain, w_cat, w_out, conv_rows, head_rows, spread, chan,
            ),
            [full(width), full(width), pl.BlockSpec((16, SPAN), lambda i: (0, i))]
            + [whole(a) for a in (gain, w_cat, w_out, conv_rows, head_rows, spread, chan)],
            (
                shape(rows, width, dtype=bf16),
                shape(rows, conv_width),
                shape(rows, inner),
                shape(rows, LANES),
                shape(rows, conv_width),
                shape(rows, inner),
                shape(rows, inner),
                shape(spans, states, inner, dtype=bf16),
                shape(spans, 2, SPAN),
            ),
            [
                full(width), full(conv_width), full(inner), full(LANES), full(conv_width),
                full(inner), full(inner),
                pl.BlockSpec((1, states, inner), lambda i: (i, 0, 0)),
                pl.BlockSpec((1, 2, SPAN), lambda i: (i, 0, 0)),
            ],
            [pltpu.VMEM((SPAN + 8, conv_width), f32), pltpu.VMEM((states, inner), f32)],
            20_000_000_000,
        )

    def tensor_small(sums):
        for step in steps_of(n_tensor):
            sums = sums + lax.ppermute(sums, "tensor", partners(n_tensor, step))
        return sums

    def gate(half, sums, gate_in, y_flat, grad_in, normed, before):
        base = half * half_spans
        full = lambda columns: pl.BlockSpec((SPAN, columns), lambda i, s: (base + i, 0))
        totals = (shape(2 * inner, width), shape(8, inner))
        return call(
            functools.partial(gate_kernel, inner=inner, inner_all=inner * n_tensor),
            grid,
            (place,),
            (sums, gate_in, y_flat, grad_in, cotangent, flags, normed, w_out, chan) + before,
            [
                pl.BlockSpec((1, 2, SPAN), lambda i, s: (base + i, 0, 0)),
                full(inner), full(inner), full(inner), full(width),
                pl.BlockSpec((16, SPAN), lambda i, s: (0, base + i)),
                full(width), whole(w_out), whole(chan),
            ]
            + [whole(a) for a in before],
            (
                shape(half_rows, width // 2),
                shape(half_rows, width // 2),
                shape(half_rows, inner),
                shape(half_rows, inner, dtype=bf16),
            )
            + totals,
            [local(width // 2), local(width // 2), local(inner), local(inner)]
            + [fixed(*a.shape) for a in totals],
            [],
            8_000_000_000,
        )

    def backward(half, normed, conv_in, dt_part, pre, y_flat, grad_y, grad_z, carried, before):
        base = half * half_spans
        turn = lambda i: base + half_spans - 1 - i
        full = lambda columns: pl.BlockSpec((SPAN, columns), lambda i, s: (turn(i), 0))
        totals = (shape(width // 2, conv_width), shape(width // 2 + 64, conv_width))
        return call(
            functools.partial(bwd_kernel, heads=heads, inner=inner, conv_width=conv_width),
            grid,
            (place,),
            (
                flags, normed, conv_in, dt_part, pre, y_flat, grad_y, grad_z, carried,
                w_cat, conv_rows, head_rows, spread, chan,
            )
            + before,
            [
                pl.BlockSpec((16, SPAN), lambda i, s: (0, turn(i))),
                full(width), full(conv_width), full(LANES), full(conv_width), full(inner),
                back(inner), back(inner),
                pl.BlockSpec((1, states, inner), lambda i, s: (turn(i), 0, 0)),
            ]
            + [whole(a) for a in (w_cat, conv_rows, head_rows, spread, chan)]
            + [whole(a) for a in before],
            (shape(half_rows, width // 2), shape(half_rows, width // 2)) + totals,
            [back(width // 2), back(width // 2)] + [fixed(*a.shape) for a in totals],
            [pltpu.VMEM((SPAN + 8, conv_width), f32), pltpu.VMEM((states, inner), f32)],
            20_000_000_000,
        )

    def placed(kernel, half, own, other, extras, extra_specs, dtype, before):
        base = half * half_spans
        full = lambda columns: pl.BlockSpec((SPAN, columns), lambda i, s: (base + i, 0))
        flag_spec = pl.BlockSpec((16, SPAN), lambda i, s: (0, base + i))
        specs = [
            whole(a) if spec is None else flag_spec if spec == 16 else full(spec)
            for a, spec in zip(extras, extra_specs)
        ]
        (made,) = call(
            kernel,
            grid,
            (place,),
            (own, other) + extras + before,
            [local(width // 2)] * 2 + specs + [pl.BlockSpec(memory_space=pl.ANY)] * len(before),
            (shape(rows, width, dtype=dtype),),
            [full(width)],
            [],
            3_000_000_000,
            {3 + len(extras): 0} if before else None,
        )
        return made

    normed, conv_in, gate_in, dt_part, pre, y_flat, grad_in, carried, sums = forward()
    sums = tensor_small(sums)
    sent, kept, gy_a, gz_a, *gate_sums = gate(0, sums, gate_in, y_flat, grad_in, normed, ())
    mixed_a = chip_sum(sent, kept, n_tensor)
    mixed_a, sums = together(mixed_a, sums)
    far_mixed_a = far_sum(mixed_a, n_tensor)
    sent, kept, gy_b, gz_b, *gate_sums = gate(
        1, sums, gate_in, y_flat, grad_in, normed, tuple(gate_sums)
    )
    early, gate_grad = gate_sums
    mixed_b = chip_sum(sent, kept, n_tensor)
    order_y, order_z = dp_order(n_dp, 0), dp_order(n_dp, 1)
    early_sent = half_sent(early, "dp", n_dp, order_y[0])
    mixed_b, gy_a = together(mixed_b, gy_a)
    far_mixed_b = far_sum(mixed_b, n_tensor)
    sent_a, kept_a, *bwd_sums = backward(
        0, normed, conv_in, dt_part, pre, y_flat, gy_a, gz_a, carried, ()
    )
    early_kept, sent_a = together(early, sent_a)
    early_parts = half_kept(early_kept, "dp", order_y[0]) + early_sent
    sent_a, far_mixed_a, early_parts, gy_b = together(sent_a, far_mixed_a, early_parts, gy_b)
    normed_sum_a = chip_sum(sent_a, kept_a, n_tensor)
    early_parts = axis_scatter(early_parts, "dp", n_dp, order_y[1:2])
    sent_b, kept_b, upper, below = backward(
        1, normed, conv_in, dt_part, pre, y_flat, gy_b, gz_b, carried,
        tuple(bwd_sums) + (early, gate_grad, gain),
    )
    sent_b, far_mixed_b, normed_sum_a, early_parts, upper, below = together(
        sent_b, far_mixed_b, normed_sum_a, early_parts, upper, below
    )
    far_normed_a = far_sum(normed_sum_a, n_tensor)
    normed_sum_b = chip_sum(sent_b, kept_b, n_tensor)
    upper = axis_scatter(upper, "dp", n_dp, order_y[:1])
    below = axis_scatter(below, "dp", n_dp, order_z[:1])
    normed_sum_b, upper, below = together(normed_sum_b, upper, below)
    far_normed_b = far_sum(normed_sum_b, n_tensor)
    upper = axis_scatter(upper, "dp", n_dp, order_y[1:])
    below = axis_scatter(below, "dp", n_dp, order_z[1:])
    early_parts = axis_scatter(early_parts, "dp", n_dp, order_y[2:])
    shared = tensor_small(jnp.concatenate([upper[:, inner:], below[:, inner:]], 0))
    upper = jnp.concatenate([upper[:, :inner], shared[: upper.shape[0]]], 1)
    below = jnp.concatenate([below[:, :inner], shared[upper.shape[0] :]], 1)
    output = placed(
        output_kernel, 0, far_mixed_a, chip_other(far_mixed_a, n_tensor), (hidden, flags),
        (width, 16), bf16, (),
    )
    output = placed(
        output_kernel, 1, far_mixed_b, chip_other(far_mixed_b, n_tensor), (hidden, flags),
        (width, 16), bf16, (output,),
    )
    upper, below, output = together(upper, below, output)
    early_sum = axis_gather(early_parts, "dp", n_dp, order_y)
    upper = axis_gather(upper, "dp", n_dp, order_y)
    below = axis_gather(below, "dp", n_dp, order_z)
    grad_hidden = placed(
        finish_kernel, 0, far_normed_a, chip_other(far_normed_a, n_tensor),
        (hidden, cotangent, gain), (width, width, None), f32, (),
    )
    grad_hidden = placed(
        finish_kernel, 1, far_normed_b, chip_other(far_normed_b, n_tensor),
        (hidden, cotangent, gain), (width, width, None), f32, (grad_hidden,),
    )
    top = width // 2
    small = below[top:]
    norm_rows = width // bc_width
    dt_grad = jnp.concatenate(
        [small[16 : 16 + heads, :inner], small[24 : 24 + heads, : width - inner]], 1
    )
    return (
        output,
        grad_hidden,
        small[9 : 9 + norm_rows, inner:].reshape(-1),
        jnp.concatenate([upper[:, :inner], below[:top, :inner]], 0),
        early_sum[inner:].T,
        dt_grad.T,
        jnp.concatenate([upper[:, inner:], below[:top, inner:]], 0),
        small[:taps, :inner],
        small[taps, :inner],
        small[:taps, inner:],
        small[taps, inner:],
        small[7, :heads],
        small[8, :heads],
        jnp.sum(small[5, :inner].reshape(heads, size), 1),
        small[6, :inner],
        early_sum[:inner],
    )


def solution(mesh):
    return jax.shard_map(
        functools.partial(per_device, mesh.shape["dp"], mesh.shape["tensor"]),
        mesh=mesh,
        in_specs=(
            P("dp", None),
            P("dp", None),
            P("dp"),
            P("dp"),
            P(),
            P(None, "tensor"),
            P(None, "tensor"),
            P(None, "tensor"),
            P(),
            P(None, "tensor"),
            P("tensor"),
            P(),
            P(),
            P("tensor"),
            P("tensor"),
            P("tensor"),
            P("tensor"),
            P("tensor", None),
        ),
        out_specs=(
            P("dp", None),
            P("dp", None),
            P(),
            P(None, "tensor"),
            P(None, "tensor"),
            P(None, "tensor"),
            P(),
            P(None, "tensor"),
            P("tensor"),
            P(),
            P(),
            P("tensor"),
            P("tensor"),
            P("tensor"),
            P("tensor"),
            P("tensor", None),
        ),
        check_vma=False,
    )
```
